256 devices in a mesh: pipe: 8 (over z_hi, y), expert: 8 (over z_lo, core), dp: 4 (over x).
Axes of the slice: x: 4, y: 4, z: 8 (z_hi: 2, z_lo: 4; z = z_hi * 4 + z_lo), core: 2. Of those that a mesh axis runs over, the one named last changes fastest.
Arguments:
- adjoint_out: bfloat16 [4096, 2048], P(('expert', 'dp')), may hold values from -6 to 6
- gate_probs: float32 [8, 4096, 2], P('pipe', ('expert', 'dp')), may hold values from 0.2 to 0.8
- routes: int32 [8, 4096, 2], P('pipe', ('expert', 'dp')), may hold values from 0 to 7, all different within a row; in each aligned block of 16 rows (0 to 15, 16 to 31, ..., all dimensions but the last counted through in order) at most 6 rows name the same one
- saved: bfloat16 [8, 8, 4, 8, 4, 48, 512], P('pipe', 'expert', 'dp'), may hold values from -6 to 6
- w_gate: bfloat16 [8, 8, 2048, 512], P('pipe', 'expert'), may hold values from -0.25 to 0.25
- w_up: bfloat16 [8, 8, 2048, 512], P('pipe', 'expert'), may hold values from -0.25 to 0.25
- w_down: bfloat16 [8, 8, 512, 2048], P('pipe', 'expert'), may hold values from -0.125 to 0.125
- probe: bfloat16 [8, 8, 2048, 512], P('pipe', 'expert'), may hold values from -0.125 to 0.125
Outputs:
- curvature_diag: float32 [8, 8, 2048, 512], P('pipe', 'expert', 'dp')
The draws below stay inside these ranges and needn't reach their ends.
Inputs may be any that keep to these rules, and one draw needn't show every extreme that they name: `routes`: each row names 2 different experts. In each block of 16 rows of one section (one microbatch of one device) no expert is named by more than 6 rows, and in some blocks one expert is named by exactly 6.
All inputs are finite; a program needn't handle non-finite values.
Results may differ from the reference program's by a relative error of at most 0.025.
Values may be sent and summed in bfloat16 or wider, within the bound.
A program may use at most 64 MiB of HBM per device.

```python
import math
import jax
import jax.numpy as jnp
import numpy as np
from jax import lax

D = 2048
FF_DEV = 512
TOP = 2
T_MB = 16
M = 8
SECTIONS = 8
EXPERTS = 8
REPLICAS = 4
CAP = 6
SLOTS = 48
TOKENS = 4096
N_EXPERT = 8


def levels(rng, shape, shards, smallest, largest):
    def one(dim, blocks):
        heights = jax.random.uniform(jax.random.fold_in(jax.random.fold_in(rng, 6), dim), (blocks,), jnp.float32, smallest / len(shards), largest / len(shards))
        return jnp.repeat(jnp.exp(heights), shape[dim] // blocks).reshape((-1,) + (1,) * (len(shape) - dim - 1))

    loudness = one(*shards[0])
    for cut in shards[1:]:
        loudness = loudness * one(*cut)
    return loudness


def shared_out(stream_key, own, number, rows, amount, top, most, slope):
    order = jax.random.permutation(stream_key, amount)
    crowded, usual = portions_of(amount, rows * top, most, slope, True), portions_of(amount, rows * top, most, slope, False)
    places = jnp.arange(amount)

    def named(sizes, offset_by):
        used = int((sizes > 0).sum())
        fixed = max(1, used // 4)
        passed = fixed + (places - fixed + offset_by * (used - fixed)) % max(1, amount - fixed)
        return jnp.zeros((amount,), jnp.int32).at[order[jnp.where(places < fixed, places, passed)]].set(jnp.asarray(sizes, jnp.int32))

    sizes = jnp.where(number % 4 == 0, named(crowded, number // 4), named(usual, number - number // 4 - 1))
    mixed = jax.random.permutation(jax.random.fold_in(own, 3), amount)
    donor, sink = mixed[0:amount // 2 * 2:2], mixed[1:amount // 2 * 2:2]
    slack = jnp.minimum(sizes[donor] - 1, most - sizes[sink]) // 2
    slack = jnp.where((donor == order[0]) | (sink == order[0]) | (sizes[sink] == 0), 0, jnp.maximum(slack, 0))
    passed = jax.random.randint(jax.random.fold_in(own, 4), (amount // 2,), 0, 1 << 20) % (slack + 1)
    sizes = sizes.at[donor].add(-passed).at[sink].add(passed)
    members = jnp.searchsorted(jnp.cumsum(sizes), jnp.arange(rows * top), side="right").astype(jnp.int32)
    grid = members.reshape(top, rows).T
    grid = grid[jax.random.permutation(jax.random.fold_in(own, 1), rows)]
    offset_by = jax.random.randint(jax.random.fold_in(own, 2), (rows, 1), 0, top)
    return jnp.take_along_axis(grid, (jnp.arange(top)[None, :] + offset_by) % top, axis=1)


def portions_of(count, total, limit, skew, full):
    portions = [(1 << 20) // math.isqrt(standing ** skew) + 1 for standing in range(1, count + 1)]
    largest = limit if full else min(limit, max(-(-total // count), total * portions[0] // sum(portions)))
    least = 1 if total - largest >= count - 1 else 0
    holding, surplus = [largest] + [least] * (count - 1), total - largest - least * (count - 1)
    while surplus > 0:
        free = [i for i in range(1, count) if holding[i] < largest] or [i for i in range(1, count) if holding[i] < limit]
        pool, budget = sum([portions[i] for i in free]), surplus
        for i in free:
            extra = min(limit - holding[i], max(1, budget * portions[i] // pool), surplus)
            holding[i] = holding[i] + extra
            surplus = surplus - extra
    return np.array(holding)


def centred(own_key, dims, spread, reach, split=(), kind=jnp.bfloat16):
    entries = jax.random.normal(own_key, dims, jnp.float32) * spread
    if len(split) > 0:
        entries = levels(own_key, dims, split, -0.22, 0.18) * entries
    return jnp.clip(entries, min=-reach, max=reach).astype(kind)


def setup_inputs(seed: int = 0) -> dict:
    key_of = jax.random.split(jax.random.key(seed), 9)
    adjoint_out = centred(key_of[0], (TOKENS, D), 1.0, 6.0, ((0, 32),))
    gate_probs = jnp.clip(0.2 + 0.6 * jax.random.uniform(key_of[1], (SECTIONS, TOKENS, TOP), jnp.float32) ** levels(key_of[1], (SECTIONS, TOKENS, TOP), ((0, 8), (1, 32)), -0.2, 0.2), 0.2, 0.8)
    routes_keys = jax.random.split(jax.random.fold_in(key_of[2], 1), SECTIONS * TOKENS // T_MB)
    routes_turns = jax.random.permutation(jax.random.fold_in(key_of[2], 3), SECTIONS * TOKENS // T_MB)
    routes = jax.vmap(lambda own, number: shared_out(jax.random.fold_in(key_of[2], 2), own, number, T_MB, EXPERTS, TOP, CAP, 1))(routes_keys, routes_turns).reshape((SECTIONS, TOKENS, TOP))
    saved = centred(key_of[3], (SECTIONS, EXPERTS, REPLICAS, M, 4, SLOTS, FF_DEV), 1.0, 6.0, ((0, 8), (1, 8), (2, 4)))
    w_gate = centred(key_of[4], (SECTIONS, EXPERTS, D, FF_DEV), FF_DEV ** -0.5, 0.25, ((0, 8), (1, 8)))
    w_up = centred(key_of[5], (SECTIONS, EXPERTS, D, FF_DEV), FF_DEV ** -0.5, 0.25, ((0, 8), (1, 8)))
    w_down = centred(key_of[6], (SECTIONS, EXPERTS, FF_DEV, D), D ** -0.5, 0.125, ((0, 8), (1, 8)))
    probe = centred(key_of[7], (SECTIONS, EXPERTS, D, FF_DEV), D ** -0.5, 0.125, ((0, 8), (1, 8)))
    return dict(adjoint_out=adjoint_out, gate_probs=gate_probs, routes=routes, saved=saved, w_gate=w_gate, w_up=w_up, w_down=w_down, probe=probe)


def contract_last(left, right):
    return lax.dot_general(left, right, (((1,), (1,)), ((), ())), preferred_element_type=jnp.float32)


def contract_first(left, right):
    return lax.dot_general(left, right, (((0,), (0,)), ((), ())), preferred_element_type=jnp.float32)


def expert_terms(pre_acts, adjoint_rows, tangent_rows, w_down, probe):
    pre_gate = pre_acts[0].astype(jnp.float32)
    pre_up = pre_acts[1].astype(jnp.float32)
    tangent_gate = pre_acts[2].astype(jnp.float32)
    tangent_up = pre_acts[3].astype(jnp.float32)
    gate_sigmoid = jax.nn.sigmoid(pre_gate)
    silu_out = pre_gate * gate_sigmoid
    first_slope = gate_sigmoid * (1.0 + pre_gate * (1.0 - gate_sigmoid))
    second_slope = gate_sigmoid * (1.0 - gate_sigmoid) * (2.0 + pre_gate * (1.0 - 2.0 * gate_sigmoid))
    hidden = (silu_out * pre_up).astype(jnp.bfloat16)
    hidden_dot = (first_slope * tangent_gate * pre_up + silu_out * tangent_up).astype(jnp.bfloat16)
    grad_hidden = contract_last(adjoint_rows, w_down)
    grad_hidden_dot = contract_last(tangent_rows, w_down) + jnp.dot(adjoint_rows, probe, preferred_element_type=jnp.float32)
    grad_gate = (grad_hidden * pre_up * first_slope).astype(jnp.bfloat16)
    grad_up = (grad_hidden * silu_out).astype(jnp.bfloat16)
    grad_gate_dot = (grad_hidden_dot * pre_up * first_slope + grad_hidden * tangent_up * first_slope
                     + grad_hidden * pre_up * second_slope * tangent_gate).astype(jnp.bfloat16)
    grad_up_dot = (grad_hidden_dot * silu_out + grad_hidden * first_slope * tangent_gate).astype(jnp.bfloat16)
    return hidden, hidden_dot, grad_gate, grad_up, grad_gate_dot, grad_up_dot


def input_grads(grad_gate, grad_up, w_gate, w_up):
    return (contract_last(grad_gate, w_gate) + contract_last(grad_up, w_up)).astype(jnp.bfloat16)


def reference(adjoint_out, gate_probs, routes, saved, w_gate, w_up, w_down, probe):
    capacity = SLOTS // N_EXPERT
    rows_device = M * T_MB
    token_ids = jnp.arange(TOKENS, dtype=jnp.int32)
    device = token_ids // rows_device
    source = device // REPLICAS
    replica = device % REPLICAS
    micro_ids = (token_ids % rows_device) // T_MB
    expert_ids = jnp.arange(EXPERTS, dtype=jnp.int32)
    total_slots = EXPERTS * REPLICAS * M * SLOTS
    expert_rows = REPLICAS * M * SLOTS
    adjoint = adjoint_out
    tangent = jnp.zeros_like(adjoint_out)
    results = []
    for section_index in range(SECTIONS - 1, -1, -1):
        chosen = routes[section_index]
        onehot = (chosen[:, :, None] == expert_ids).astype(jnp.int32)
        blocks = onehot.reshape(TOKENS // T_MB, T_MB * TOP, EXPERTS)
        before = jnp.cumsum(blocks, axis=1) - blocks
        position = jnp.sum(before * blocks, axis=2).reshape(TOKENS, TOP)
        target = ((chosen * REPLICAS + replica[:, None]) * M + micro_ids[:, None]) * SLOTS + source[:, None] * capacity + position
        target = target.reshape(-1).astype(jnp.int32)
        gate_scale = gate_probs[section_index][:, :, None]
        adjoint_pick = (gate_scale * adjoint.astype(jnp.float32)[:, None, :]).astype(jnp.bfloat16).reshape(-1, D)
        tangent_pick = (gate_scale * tangent.astype(jnp.float32)[:, None, :]).astype(jnp.bfloat16).reshape(-1, D)
        adjoint_slots = jnp.zeros((total_slots, D), jnp.bfloat16).at[target].set(adjoint_pick).reshape(EXPERTS, expert_rows, D)
        tangent_slots = jnp.zeros((total_slots, D), jnp.bfloat16).at[target].set(tangent_pick).reshape(EXPERTS, expert_rows, D)
        pre_acts = jnp.transpose(saved[section_index], (0, 3, 1, 2, 4, 5)).reshape(EXPERTS, 4, expert_rows, FF_DEV)

        def one_expert(expert_items):
            pre_e, adjoint_e, tangent_e, gate_e, up_e, down_e, probe_e = expert_items
            hidden, hidden_dot, grad_gate, grad_up, grad_gate_dot, grad_up_dot = expert_terms(pre_e, adjoint_e, tangent_e, down_e, probe_e)
            back_adjoint = input_grads(grad_gate, grad_up, gate_e, up_e)
            back_tangent = input_grads(grad_gate_dot, grad_up_dot, gate_e, up_e)
            curvature = probe_e.astype(jnp.float32) * (contract_first(adjoint_e, hidden_dot) + contract_first(tangent_e, hidden))
            return back_adjoint, back_tangent, curvature

        back_adjoint, back_tangent, curvature = lax.map(
            one_expert,
            (pre_acts, adjoint_slots, tangent_slots, w_gate[section_index], w_up[section_index], w_down[section_index], probe[section_index]))
        returned = back_adjoint.reshape(-1, D)[target].reshape(TOKENS, TOP, D).astype(jnp.float32)
        returned_dot = back_tangent.reshape(-1, D)[target].reshape(TOKENS, TOP, D).astype(jnp.float32)
        adjoint = (adjoint.astype(jnp.float32) + jnp.sum(returned, axis=1)).astype(jnp.bfloat16)
        tangent = (tangent.astype(jnp.float32) + jnp.sum(returned_dot, axis=1)).astype(jnp.bfloat16)
        results.append(curvature)
    return jnp.stack(results[::-1])
```

```python
import functools

import jax
import jax.numpy as jnp
import numpy as np
from jax import lax
from jax.experimental import pallas as pl
from jax.experimental.pallas import tpu as pltpu
from jax.sharding import PartitionSpec as P

M = 8
T_MB = 16
TOP = 2
QUARTERS = 4
CHUNKS = 2
KINDS = 2
MESH = pl.DeviceIdType.MESH
F32 = jnp.float32
BF16 = jnp.bfloat16


def dot(left, right, dims):
    return lax.dot_general(left, right, (dims, ((), ())), preferred_element_type=F32)


def wait_bytes(view, sem):
    pltpu.make_async_copy(view, view, sem).wait()


def relay_kernel(
    sizes,
    target_ref,
    weight_ref,
    order_ref,
    unorder_ref,
    adjoint_ref,
    saved_ref,
    gate_ref,
    up_ref,
    down_ref,
    probe_ref,
    out_ref,
    target_above,
    token_in,
    token_now,
    pick_send,
    pick_recv,
    back_send,
    back_recv,
    pick_rows,
    block_rows,
    hidden_rows,
    factors,
    grads,
    total,
    table_send_sem,
    table_recv_sem,
    token_send_sem,
    token_recv_sem,
    pick_send_sem,
    pick_recv_sem,
    back_send_sem,
    back_recv_sem,
    block_send_sem,
    block_recv_sem,
    hidden_send_sem,
    hidden_recv_sem,
):
    stages, experts, replicas, capacity = sizes
    stage = lax.axis_index("pipe")
    expert = lax.axis_index("expert")
    replica = lax.axis_index("dp")
    below = lax.rem(stage + stages - 1, stages)
    above = lax.rem(stage + 1, stages)
    is_top = stage == stages - 1
    is_bottom = stage == 0
    slots = experts * capacity
    wire = QUARTERS * KINDS * capacity
    lanes = pick_send.shape[-1]
    quarter = lanes * CHUNKS
    width = gate_ref.shape[1]
    pair = KINDS * slots
    block = QUARTERS // replicas

    barrier = pltpu.get_barrier_semaphore()

    def greet(peer, carry):
        pl.semaphore_signal(
            barrier, inc=1, device_id={"pipe": below, "expert": peer}, device_id_type=MESH
        )
        pl.semaphore_signal(
            barrier, inc=1, device_id={"pipe": above, "expert": peer}, device_id_type=MESH
        )
        return carry

    lax.fori_loop(0, experts, greet, 0)
    for step in range(1, experts):
        pl.semaphore_signal(
            barrier,
            inc=1,
            device_id={"expert": lax.rem(expert + step, experts)},
            device_id_type=MESH,
        )
    for step in range(1, replicas):
        pl.semaphore_signal(
            barrier,
            inc=1,
            device_id={"dp": lax.rem(replica + step, replicas)},
            device_id_type=MESH,
        )
    pl.semaphore_wait(barrier, 2 * experts + experts - 1 + replicas - 1)

    table_copy = pltpu.make_async_remote_copy(
        src_ref=target_ref,
        dst_ref=target_above,
        send_sem=table_send_sem,
        recv_sem=table_recv_sem,
        device_id={"pipe": below},
        device_id_type=MESH,
    )

    @pl.when(jnp.logical_not(is_bottom))
    def _():
        table_copy.start()

    @pl.when(jnp.logical_not(is_top))
    def _():
        table_copy.wait_recv()

    rows = lax.broadcasted_iota(jnp.int32, (experts * wire, 128), 0)

    def matches(table, micro):
        pair_rows = table[micro]
        return rows == pair_rows[0:1, :], rows == pair_rows[1:2, :]

    def curvature(micro):
        wait_bytes(block_rows.at[micro], block_recv_sem.at[micro])
        wait_bytes(hidden_rows.at[micro, pl.ds(0, replicas - 1)], hidden_recv_sem.at[micro])
        right = hidden_rows[micro].reshape(replicas * pair, width)
        for chunk in range(CHUNKS):
            for part in range(block):
                left = block_rows[micro, chunk, :, part * pair : (part + 1) * pair, :]
                found = dot(left.reshape(replicas * pair, lanes), right, ((0,), (0,)))
                start = part * quarter + chunk * lanes
                here = slice(start, start + lanes)

                @pl.when(micro == 0)
                def _():
                    total[here, :] = found

                @pl.when(micro > 0)
                def _():
                    total[here, :] = total[here, :] + found

    def advance(micro, carry):
        first, second = matches(target_ref, micro)
        weights = weight_ref[micro]
        placing = jnp.where(first | second, 1.0, 0.0).astype(BF16)
        scale = jnp.sum(
            jnp.where(first, weights[0:1, :], 0.0) + jnp.where(second, weights[1:2, :], 0.0),
            axis=1,
            keepdims=True,
        )

        for chunk in range(CHUNKS):

            @pl.when(is_top)
            def _():
                row_start = pl.multiple_of(micro * T_MB, T_MB)
                for part in range(QUARTERS):
                    start = part * quarter + chunk * lanes
                    base = part * KINDS * T_MB
                    token_now[micro, chunk, base : base + T_MB, :] = adjoint_ref[
                        pl.ds(row_start, T_MB), start : start + lanes
                    ]
                    token_now[micro, chunk, base + T_MB : base + 2 * T_MB, :] = jnp.zeros(
                        (T_MB, lanes), BF16
                    )

            @pl.when(jnp.logical_not(is_top))
            def _():
                above_first, above_second = matches(target_above, micro)
                merging = jnp.where(above_first | above_second, 1.0, 0.0).astype(BF16)
                wait_bytes(token_in.at[micro, chunk], token_recv_sem.at[micro, chunk])
                wait_bytes(back_recv.at[micro, chunk], back_recv_sem.at[micro, chunk])
                returned = back_recv[micro, chunk].reshape(experts * wire, lanes)
                token_now[micro, chunk] = (
                    token_in[micro, chunk].astype(F32) + dot(merging, returned, ((0,), (0,)))
                ).astype(BF16)

            picked = dot(placing, token_now[micro, chunk], ((1,), (0,))) * scale
            pick_send[micro, chunk] = picked.astype(BF16).reshape(experts, wire, lanes)
            for step in range(1, experts):
                peer = lax.rem(expert + step, experts)
                pltpu.make_async_remote_copy(
                    src_ref=pick_send.at[micro, chunk, peer],
                    dst_ref=pick_recv.at[micro, chunk, expert],
                    send_sem=pick_send_sem.at[micro],
                    recv_sem=pick_recv_sem.at[micro, chunk],
                    device_id={"expert": peer},
                    device_id_type=MESH,
                ).start()
            pltpu.make_async_copy(
                pick_send.at[micro, chunk, expert],
                pick_recv.at[micro, chunk, expert],
                pick_recv_sem.at[micro, chunk],
            ).start()

            @pl.when(jnp.logical_not(is_bottom))
            def _():
                pltpu.make_async_remote_copy(
                    src_ref=token_now.at[micro, chunk],
                    dst_ref=token_in.at[micro, chunk],
                    send_sem=token_send_sem.at[micro],
                    recv_sem=token_recv_sem.at[micro, chunk],
                    device_id={"pipe": below},
                    device_id_type=MESH,
                ).start()

        pre_gate = saved_ref[micro, 0].astype(F32)
        pre_up = saved_ref[micro, 1].astype(F32)
        tangent_gate = saved_ref[micro, 2].astype(F32)
        tangent_up = saved_ref[micro, 3].astype(F32)
        sigmoid = jax.nn.sigmoid(pre_gate)
        silu = pre_gate * sigmoid
        slope = sigmoid * (1.0 + pre_gate * (1.0 - sigmoid))
        bend = sigmoid * (1.0 - sigmoid) * (2.0 + pre_gate * (1.0 - 2.0 * sigmoid))
        hidden_rows[micro, replica, 0:slots, :] = (
            slope * tangent_gate * pre_up + silu * tangent_up
        ).astype(BF16)
        hidden_rows[micro, replica, slots:pair, :] = (silu * pre_up).astype(BF16)
        for step in range(1, replicas):
            pltpu.make_async_remote_copy(
                src_ref=hidden_rows.at[micro, replica],
                dst_ref=hidden_rows.at[micro, replica],
                send_sem=hidden_send_sem.at[micro],
                recv_sem=hidden_recv_sem.at[micro],
                device_id={"dp": lax.rem(replica + step, replicas)},
                device_id_type=MESH,
            ).start()
        factors[0] = pre_up * slope
        factors[1] = silu
        factors[2] = tangent_up * slope + pre_up * bend * tangent_gate
        factors[3] = slope * tangent_gate

        @pl.when(micro > 0)
        def _():
            curvature(micro - 1)

        for chunk in range(CHUNKS):
            wait_bytes(pick_recv.at[micro, chunk], pick_recv_sem.at[micro, chunk])
            received = pick_recv[micro, chunk].reshape(experts * wire, lanes)
            ordered = dot(order_ref[...], received, ((1,), (0,))).astype(BF16)
            pick_rows[micro, chunk] = ordered
            for step in range(1, replicas):
                peer = lax.rem(replica + step, replicas)
                pltpu.make_async_remote_copy(
                    src_ref=pick_rows.at[micro, chunk, pl.ds(peer * (block * pair), block * pair)],
                    dst_ref=block_rows.at[micro, chunk, replica],
                    send_sem=block_send_sem.at[micro],
                    recv_sem=block_recv_sem.at[micro],
                    device_id={"dp": peer},
                    device_id_type=MESH,
                ).start()
            pltpu.make_async_copy(
                pick_rows.at[micro, chunk, pl.ds(replica * (block * pair), block * pair)],
                block_rows.at[micro, chunk, replica],
                block_recv_sem.at[micro],
            ).start()

            @pl.when(jnp.logical_not(is_bottom))
            def _():
                both = jnp.concatenate(
                    [ordered[part * pair : (part + 1) * pair, :] for part in range(QUARTERS)],
                    axis=1,
                )
                starts = [part * quarter + chunk * lanes for part in range(QUARTERS)]
                down = jnp.concatenate(
                    [down_ref[:, start : start + lanes] for start in starts], axis=1
                )
                aside = jnp.concatenate(
                    [probe_ref[start : start + lanes, :] for start in starts], axis=0
                )
                main = dot(both, down, ((1,), (1,)))
                extra = dot(both[0:slots, :], aside, ((1,), (0,)))
                if chunk == 0:
                    grads[0] = main[0:slots, :]
                    grads[1] = main[slots:pair, :] + extra
                else:
                    grads[0] = grads[0] + main[0:slots, :]
                    grads[1] = grads[1] + (main[slots:pair, :] + extra)

        @pl.when(jnp.logical_not(is_bottom))
        def _():
            grad = grads[0]
            grad_dot = grads[1]
            left = jnp.concatenate(
                [
                    jnp.concatenate(
                        [
                            (grad * factors[0]).astype(BF16),
                            (grad_dot * factors[0] + grad * factors[2]).astype(BF16),
                        ],
                        axis=0,
                    ),
                    jnp.concatenate(
                        [
                            (grad * factors[1]).astype(BF16),
                            (grad_dot * factors[1] + grad * factors[3]).astype(BF16),
                        ],
                        axis=0,
                    ),
                ],
                axis=1,
            )
            for chunk in range(CHUNKS):
                starts = [part * quarter + chunk * lanes for part in range(QUARTERS)]
                right = jnp.concatenate(
                    [
                        jnp.concatenate(
                            [gate_ref[start : start + lanes, :] for start in starts], axis=0
                        ),
                        jnp.concatenate(
                            [up_ref[start : start + lanes, :] for start in starts], axis=0
                        ),
                    ],
                    axis=1,
                )
                back = dot(left, right, ((1,), (1,))).astype(BF16)
                stacked = jnp.concatenate(
                    [back[:, part * lanes : (part + 1) * lanes] for part in range(QUARTERS)],
                    axis=0,
                )
                back_send[micro, chunk] = (
                    dot(unorder_ref[...], stacked, ((1,), (0,)))
                    .astype(BF16)
                    .reshape(experts, wire, lanes)
                )
                for step in range(experts):
                    peer = lax.rem(expert + step, experts)
                    pltpu.make_async_remote_copy(
                        src_ref=back_send.at[micro, chunk, peer],
                        dst_ref=back_recv.at[micro, chunk, expert],
                        send_sem=back_send_sem.at[micro],
                        recv_sem=back_recv_sem.at[micro, chunk],
                        device_id={"pipe": below, "expert": peer},
                        device_id_type=MESH,
                    ).start()

        return carry

    lax.fori_loop(0, M, advance, 0)
    curvature(M - 1)
    rows_here = block * quarter
    start = pl.multiple_of(replica * rows_here, rows_here)
    out_ref[...] = probe_ref[pl.ds(start, rows_here), :].astype(F32) * total[...]

    def settle(micro, carry):
        wait_bytes(pick_send.at[micro, :, pl.ds(0, experts - 1)], pick_send_sem.at[micro])
        wait_bytes(hidden_rows.at[micro, pl.ds(0, replicas - 1)], hidden_send_sem.at[micro])
        wait_bytes(
            block_rows.at[micro, :, pl.ds(0, replicas - 1)], block_send_sem.at[micro]
        )

        @pl.when(jnp.logical_not(is_bottom))
        def _():
            wait_bytes(back_send.at[micro], back_send_sem.at[micro])
            wait_bytes(token_now.at[micro], token_send_sem.at[micro])

        return carry

    lax.fori_loop(0, M, settle, 0)

    @pl.when(jnp.logical_not(is_bottom))
    def _():
        table_copy.wait_send()


def row_orders(experts, capacity):
    slots = experts * capacity
    count = QUARTERS * KINDS * slots
    order = np.zeros((count, count), np.float32)
    for kind in range(QUARTERS * KINDS):
        for source in range(experts):
            for slot in range(capacity):
                order[
                    kind * slots + source * capacity + slot,
                    (source * QUARTERS * KINDS + kind) * capacity + slot,
                ] = 1.0
    return order


def pick_tables(routes, probs, capacity):
    picks = T_MB * TOP
    flat = routes.reshape(M, picks)
    index = jnp.arange(picks, dtype=jnp.int32)
    earlier = index[None, :] < index[:, None]
    same = flat[:, :, None] == flat[:, None, :]
    position = jnp.sum((same & earlier[None]).astype(jnp.int32), axis=2)
    parts = QUARTERS * KINDS
    base = (flat * (parts * capacity) + position).reshape(M, T_MB, TOP).transpose(0, 2, 1)
    offset = jnp.arange(parts, dtype=jnp.int32) * capacity
    target = (base[:, :, None, :] + offset[None, None, :, None]).reshape(M, TOP, parts * T_MB)
    weight = jnp.broadcast_to(
        probs.reshape(M, T_MB, TOP).transpose(0, 2, 1)[:, :, None, :], (M, TOP, parts, T_MB)
    ).reshape(M, TOP, parts * T_MB)
    return target, weight


def per_device(adjoint_out, gate_probs, routes, saved, w_gate, w_up, w_down, probe):
    stages = lax.axis_size("pipe")
    experts = lax.axis_size("expert")
    replicas = lax.axis_size("dp")
    slots = saved.shape[5]
    capacity = slots // experts
    model = adjoint_out.shape[1]
    width = w_gate.shape[3]
    lanes = model // QUARTERS // CHUNKS
    wire = QUARTERS * KINDS * capacity
    tokens = QUARTERS * KINDS * T_MB
    pair = KINDS * slots
    block = QUARTERS // replicas
    target, weight = pick_tables(routes[0], gate_probs[0], capacity)
    order = row_orders(experts, capacity)
    vmem = pl.BlockSpec(memory_space=pltpu.VMEM)
    dma = pltpu.SemaphoreType.DMA
    found = pl.pallas_call(
        functools.partial(relay_kernel, (stages, experts, replicas, capacity)),
        out_shape=jax.ShapeDtypeStruct((model // replicas, width), F32),
        in_specs=[vmem] * 10,
        out_specs=vmem,
        scratch_shapes=[
            pltpu.VMEM((M, TOP, tokens), jnp.int32),
            pltpu.VMEM((M, CHUNKS, tokens, lanes), BF16),
            pltpu.VMEM((M, CHUNKS, tokens, lanes), BF16),
            pltpu.VMEM((M, CHUNKS, experts, wire, lanes), BF16),
            pltpu.VMEM((M, CHUNKS, experts, wire, lanes), BF16),
            pltpu.VMEM((M, CHUNKS, experts, wire, lanes), BF16),
            pltpu.VMEM((M, CHUNKS, experts, wire, lanes), BF16),
            pltpu.VMEM((M, CHUNKS, QUARTERS * pair, lanes), BF16),
            pltpu.VMEM((M, CHUNKS, replicas, block * pair, lanes), BF16),
            pltpu.VMEM((M, replicas, pair, width), BF16),
            pltpu.VMEM((4, slots, width), F32),
            pltpu.VMEM((2, slots, width), F32),
            pltpu.VMEM((model // replicas, width), F32),
            dma,
            dma,
            dma((M,)),
            dma((M, CHUNKS)),
            dma((M,)),
            dma((M, CHUNKS)),
            dma((M,)),
            dma((M, CHUNKS)),
            dma((M,)),
            dma((M,)),
            dma((M,)),
            dma((M,)),
        ],
        compiler_params=pltpu.CompilerParams(
            collective_id=0, has_side_effects=True, vmem_limit_bytes=60 * 1024 * 1024
        ),
        name="relay",
    )(
        target,
        weight,
        jnp.asarray(order, BF16),
        jnp.asarray(order.T, BF16),
        adjoint_out,
        saved[0, 0, 0],
        w_gate[0, 0],
        w_up[0, 0],
        w_down[0, 0],
        probe[0, 0],
    )
    return found[None, None]


def solution(mesh):
    return jax.shard_map(
        per_device,
        mesh=mesh,
        in_specs=(
            P(("expert", "dp"), None),
            P("pipe", ("expert", "dp"), None),
            P("pipe", ("expert", "dp"), None),
            P("pipe", "expert", "dp", None, None, None, None),
            P("pipe", "expert", None, None),
            P("pipe", "expert", None, None),
            P("pipe", "expert", None, None),
            P("pipe", "expert", None, None),
        ),
        out_specs=P("pipe", "expert", "dp", None),
        check_vma=False,
    )
```

```python
import functools

import jax
import jax.numpy as jnp
import numpy as np
from jax import lax
from jax.experimental import pallas as pl
from jax.experimental.pallas import tpu as pltpu
from jax.sharding import PartitionSpec as P

M = 8
T_MB = 16
TOP = 2
KINDS = 2
CHUNKS = 2
PARTS = 4
MESH = pl.DeviceIdType.MESH
F32 = jnp.float32
BF16 = jnp.bfloat16


def dot(left, right, dims):
    return lax.dot_general(left, right, (dims, ((), ())), preferred_element_type=F32)


def wait_bytes(view, sem):
    pltpu.make_async_copy(view, view, sem).wait()


def relay_kernel(
    sizes,
    target_ref,
    weight_ref,
    order_ref,
    unorder_ref,
    adjoint_ref,
    saved_ref,
    gate_ref,
    up_ref,
    down_ref,
    probe_ref,
    out_ref,
    target_own,
    weight_own,
    target_above,
    token_in,
    token_now,
    pick_send,
    pick_recv,
    back_send,
    back_recv,
    pick_rows,
    block_rows,
    hidden_rows,
    factors,
    grads,
    total,
    down_turned,
    inner_turned,
    placing_ref,
    merging_ref,
    scale_ref,
    table_send_sem,
    table_recv_sem,
    token_send_sem,
    token_recv_sem,
    pick_send_sem,
    pick_recv_sem,
    back_send_sem,
    back_recv_sem,
    block_send_sem,
    block_recv_sem,
    hidden_send_sem,
    hidden_recv_sem,
):
    stages, experts, replicas, capacity = sizes
    stage = lax.axis_index("pipe")
    expert = lax.axis_index("expert")
    replica = lax.axis_index("dp")
    below = lax.rem(stage + stages - 1, stages)
    above = lax.rem(stage + 1, stages)
    is_top = stage == stages - 1
    is_bottom = stage == 0
    adds_own = stage == stages // 2
    gets_sums = stage == stages // 2 - 1
    back_stage = jnp.where(adds_own, stage, below)
    is_lower = stage < stages // 2
    mirror = experts - 1 - expert
    source = jnp.where(is_lower, mirror, expert)
    expert_below = jnp.where(adds_own, mirror, expert)
    slots = experts * capacity
    wire = PARTS * capacity
    lanes = pick_send.shape[-1]
    span = PARTS * lanes
    width = gate_ref.shape[1]
    block_parts = CHUNKS * PARTS // replicas
    block = block_parts * slots

    expert_peers = [lax.rem(expert + step, experts) for step in range(experts)]
    replica_peers = [lax.rem(replica + step, replicas) for step in range(replicas)]

    barrier = pltpu.get_barrier_semaphore()

    def greet(peer, carry):
        for other in (below, above):
            pl.semaphore_signal(
                barrier, inc=1, device_id={"pipe": other, "expert": peer}, device_id_type=MESH
            )
        return carry

    lax.fori_loop(0, experts, greet, 0)
    for step in range(1, experts):
        pl.semaphore_signal(
            barrier,
            inc=1,
            device_id={"expert": expert_peers[step]},
            device_id_type=MESH,
        )
    for step in range(1, replicas):
        pl.semaphore_signal(
            barrier,
            inc=1,
            device_id={"dp": replica_peers[step]},
            device_id_type=MESH,
        )
    pl.semaphore_wait(barrier, 2 * experts + experts - 1 + replicas - 1)

    def table_copy(source_ref, landing_ref, index, device):
        return pltpu.make_async_remote_copy(
            src_ref=source_ref,
            dst_ref=landing_ref,
            send_sem=table_send_sem.at[index],
            recv_sem=table_recv_sem.at[index],
            device_id=device,
            device_id_type=MESH,
        )

    below_copy = table_copy(
        target_ref,
        target_above,
        0,
        {"pipe": below, "expert": jnp.where(stage <= stages // 2, mirror, expert)},
    )
    mirror_copies = [
        table_copy(target_ref, target_own, 1, {"expert": mirror}),
        table_copy(weight_ref, weight_own, 2, {"expert": mirror}),
    ]

    @pl.when(jnp.logical_not(is_bottom))
    def _():
        below_copy.start()

    @pl.when(is_lower)
    def _():
        for copy in mirror_copies:
            copy.start()
        for copy in mirror_copies:
            copy.wait_recv()

    @pl.when(jnp.logical_not(is_lower))
    def _():
        target_own[...] = target_ref[...]
        weight_own[...] = weight_ref[...]

    @pl.when(jnp.logical_not(is_top))
    def _():
        below_copy.wait_recv()

    rows = lax.broadcasted_iota(jnp.int32, (experts * wire, PARTS * T_MB), 0)

    def matches(table, micro):
        pair_rows = table[micro]
        return rows == pair_rows[0:1, :], rows == pair_rows[1:2, :]

    def onehot(first, second):
        return jnp.where(first | second, 1.0, 0.0).astype(BF16)

    def curvature(micro, kind):
        if kind == 0:
            wait_bytes(hidden_rows.at[micro, :, pl.ds(0, replicas - 1)], hidden_recv_sem.at[micro])
        wait_bytes(block_rows.at[micro, kind], block_recv_sem.at[micro, kind])
        right = hidden_rows[micro, kind].reshape(replicas * slots, width)
        for part in range(block_parts):
            left = block_rows[micro, kind, :, part * slots : (part + 1) * slots, :]
            found = dot(left.reshape(replicas * slots, lanes), right, ((0,), (0,)))
            here = slice(part * lanes, (part + 1) * lanes)
            total[here, :] = total[here, :] + found

    def merge(merging, base, micro, kind, chunk):
        wait_bytes(back_recv.at[micro, kind, chunk], back_recv_sem.at[micro, kind, chunk])
        returned = back_recv[micro, kind, chunk].reshape(experts * wire, lanes)
        token_now[micro, kind, chunk] = (
            base.astype(F32) + dot(merging, returned, ((0,), (0,)))
        ).astype(BF16)

    def forward(micro, kind, chunk):
        pltpu.make_async_remote_copy(
            src_ref=token_now.at[micro, kind, chunk],
            dst_ref=token_in.at[micro, kind, chunk],
            send_sem=token_send_sem.at[micro],
            recv_sem=token_recv_sem.at[micro, kind, chunk],
            device_id={"pipe": below, "expert": expert_below},
            device_id_type=MESH,
        ).start()

    def add_own(micro, kind):
        merging = onehot(*matches(target_own, micro))
        for chunk in range(CHUNKS):
            merge(merging, token_now[micro, kind, chunk], micro, kind, chunk)
            forward(micro, kind, chunk)

    def tables(micro):
        first, second = matches(target_own, micro)
        weights = weight_own[micro]
        placing_ref[...] = onehot(first, second)
        scale_ref[...] = jnp.broadcast_to(
            jnp.sum(
                jnp.where(first, weights[0:1, :], 0.0) + jnp.where(second, weights[1:2, :], 0.0),
                axis=1,
                keepdims=True,
            ),
            scale_ref.shape,
        )
        merging_ref[...] = onehot(*matches(target_above, micro))

    def hand_out(micro, kind):
        for chunk in range(CHUNKS):

            @pl.when(is_top)
            def _():
                row_start = pl.multiple_of(micro * T_MB, T_MB)
                for part in range(PARTS):
                    start = chunk * span + part * lanes
                    base = part * T_MB
                    if kind == 0:
                        piece = adjoint_ref[pl.ds(row_start, T_MB), start : start + lanes]
                    else:
                        piece = jnp.zeros((T_MB, lanes), BF16)
                    token_now[micro, kind, chunk, base : base + T_MB, :] = piece

            @pl.when(jnp.logical_not(is_top))
            def _():
                wait_bytes(token_in.at[micro, kind, chunk], token_recv_sem.at[micro, kind, chunk])

            @pl.when(gets_sums)
            def _():
                token_now[micro, kind, chunk] = token_in[micro, kind, chunk]

            @pl.when(jnp.logical_not(is_top | gets_sums))
            def _():
                merge(merging_ref[...], token_in[micro, kind, chunk], micro, kind, chunk)

            picked = dot(placing_ref[...], token_now[micro, kind, chunk], ((1,), (0,)))
            picked = picked * scale_ref[...]
            pick_send[micro, kind, chunk] = picked.astype(BF16).reshape(experts, wire, lanes)
            for step in range(1, experts):
                peer = expert_peers[step]
                pltpu.make_async_remote_copy(
                    src_ref=pick_send.at[micro, kind, chunk, peer],
                    dst_ref=pick_recv.at[micro, kind, chunk, source],
                    send_sem=pick_send_sem.at[micro],
                    recv_sem=pick_recv_sem.at[micro, kind, chunk],
                    device_id={"expert": peer},
                    device_id_type=MESH,
                ).start()
            pltpu.make_async_copy(
                pick_send.at[micro, kind, chunk, expert],
                pick_recv.at[micro, kind, chunk, source],
                pick_recv_sem.at[micro, kind, chunk],
            ).start()

            @pl.when(jnp.logical_not(is_bottom | adds_own))
            def _():
                forward(micro, kind, chunk)

    def activations(micro):
        pre_gate = saved_ref[micro, 0].astype(F32)
        pre_up = saved_ref[micro, 1].astype(F32)
        tangent_gate = saved_ref[micro, 2].astype(F32)
        tangent_up = saved_ref[micro, 3].astype(F32)
        sigmoid = jax.nn.sigmoid(pre_gate)
        silu = pre_gate * sigmoid
        slope = sigmoid * (1.0 + pre_gate * (1.0 - sigmoid))
        bend = sigmoid * (1.0 - sigmoid) * (2.0 + pre_gate * (1.0 - 2.0 * sigmoid))
        hidden_rows[micro, 0, replica] = (
            slope * tangent_gate * pre_up + silu * tangent_up
        ).astype(BF16)
        hidden_rows[micro, 1, replica] = (silu * pre_up).astype(BF16)
        for step in range(1, replicas):
            pltpu.make_async_remote_copy(
                src_ref=hidden_rows.at[micro, :, replica],
                dst_ref=hidden_rows.at[micro, :, replica],
                send_sem=hidden_send_sem.at[micro],
                recv_sem=hidden_recv_sem.at[micro],
                device_id={"dp": replica_peers[step]},
                device_id_type=MESH,
            ).start()
        factors[0] = pre_up * slope
        factors[1] = silu
        factors[2] = tangent_up * slope + pre_up * bend * tangent_gate
        factors[3] = slope * tangent_gate

    def side_by_side(ordered):
        return jnp.concatenate(
            [ordered[part * slots : (part + 1) * slots, :] for part in range(PARTS)], axis=1
        )

    def take_in(micro, kind):
        for chunk in range(CHUNKS):
            columns = slice(chunk * span, (chunk + 1) * span)
            wait_bytes(pick_recv.at[micro, kind, chunk], pick_recv_sem.at[micro, kind, chunk])
            received = pick_recv[micro, kind, chunk].reshape(experts * wire, lanes)
            ordered = dot(order_ref[...], received, ((1,), (0,))).astype(BF16)
            pick_rows[micro, kind, chunk] = ordered

            @pl.when(jnp.logical_not(is_bottom))
            def _():
                main = dot(side_by_side(ordered), down_turned[columns, :], ((1,), (0,)))
                if chunk == 0:
                    grads[kind] = main + grads[1] if kind == 1 else main
                else:
                    grads[kind] = grads[kind] + main

            for step in range(replicas):
                peer = replica_peers[step]
                first_part = peer * block_parts
                rows_out = pick_rows.at[
                    micro, kind, chunk, pl.ds(lax.rem(first_part, PARTS) * slots, block)
                ]
                landing = block_rows.at[micro, kind, replica]

                @pl.when(lax.div(first_part, PARTS) == chunk)
                def _():
                    if step == 0:
                        pltpu.make_async_copy(
                            rows_out, landing, block_recv_sem.at[micro, kind]
                        ).start()
                    else:
                        pltpu.make_async_remote_copy(
                            src_ref=rows_out,
                            dst_ref=landing,
                            send_sem=block_send_sem.at[micro],
                            recv_sem=block_recv_sem.at[micro, kind],
                            device_id={"dp": peer},
                            device_id_type=MESH,
                        ).start()

    def hand_back(micro, kind):
        grad = grads[0]
        if kind == 0:
            left = [grad * factors[0], grad * factors[1]]
        else:
            grad_dot = grads[1]
            left = [
                grad_dot * factors[0] + grad * factors[2],
                grad_dot * factors[1] + grad * factors[3],
            ]
        left = jnp.concatenate([piece.astype(BF16) for piece in left], axis=1)
        for chunk in range(CHUNKS):
            columns = slice(chunk * span, (chunk + 1) * span)
            back = dot(left, inner_turned[:, columns], ((1,), (0,))).astype(BF16)
            stacked = jnp.concatenate(
                [back[:, part * lanes : (part + 1) * lanes] for part in range(PARTS)], axis=0
            )
            back_send[micro, kind, chunk] = (
                dot(unorder_ref[...], stacked, ((1,), (0,)))
                .astype(BF16)
                .reshape(experts, wire, lanes)
            )
            for step in range(1, experts + 1):
                peer = expert_peers[step % experts]
                copy = pltpu.make_async_remote_copy(
                    src_ref=back_send.at[
                        micro, kind, chunk, jnp.where(is_lower, experts - 1 - peer, peer)
                    ],
                    dst_ref=back_recv.at[micro, kind, chunk, expert],
                    send_sem=back_send_sem.at[micro],
                    recv_sem=back_recv_sem.at[micro, kind, chunk],
                    device_id={"pipe": back_stage, "expert": peer},
                    device_id_type=MESH,
                )
                if step < experts:
                    copy.start()
                else:
                    pl.when(jnp.logical_not(adds_own))(copy.start)

                    @pl.when(adds_own)
                    def _():
                        pltpu.make_async_copy(
                            back_send.at[micro, kind, chunk, expert],
                            back_recv.at[micro, kind, chunk, expert],
                            back_recv_sem.at[micro, kind, chunk],
                        ).start()

    total[...] = jnp.zeros_like(total)

    def turn_weights():
        side = min(256, down_ref.shape[1])

        def turn_down(index, carry):
            here = pl.ds(pl.multiple_of(index * side, side), side)
            down_turned[here, :] = down_ref[:, here].T
            inner_turned[0:width, here] = gate_ref[here, :].T
            inner_turned[width : 2 * width, here] = up_ref[here, :].T
            return carry

        lax.fori_loop(0, down_ref.shape[1] // side, turn_down, 0)

    def aside(micro):
        for chunk in range(CHUNKS):
            found = dot(
                side_by_side(pick_rows[micro, 0, chunk]),
                probe_ref[chunk * span : (chunk + 1) * span, :],
                ((1,), (0,)),
            )
            grads[1] = found if chunk == 0 else grads[1] + found

    def advance(micro, carry):
        hand_out(micro, 0)
        hand_out(micro, 1)

        @pl.when(is_top & (micro == 0))
        def _():
            turn_weights()

        activations(micro)

        @pl.when(micro > 0)
        def _():
            curvature(micro - 1, 0)
            curvature(micro - 1, 1)

        @pl.when(micro < M - 1)
        def _():
            tables(micro + 1)

        take_in(micro, 0)

        @pl.when(jnp.logical_not(is_bottom))
        def _():
            hand_back(micro, 0)
            aside(micro)

        @pl.when(micro == M - 1)
        def _():
            curvature(micro, 0)

        take_in(micro, 1)

        @pl.when(jnp.logical_not(is_bottom))
        def _():
            hand_back(micro, 1)

        @pl.when(adds_own)
        def _():
            add_own(micro, 0)
            add_own(micro, 1)

        return carry

    tables(0)

    @pl.when(jnp.logical_not(is_top))
    def _():
        turn_weights()

    lax.fori_loop(0, M, advance, 0)
    curvature(M - 1, 1)
    rows_here = block_parts * lanes
    start = pl.multiple_of(replica * rows_here, rows_here)
    out_ref[...] = probe_ref[pl.ds(start, rows_here), :].astype(F32) * total[...]

    def settle(micro, carry):
        wait_bytes(pick_send.at[micro, :, :, pl.ds(0, experts - 1)], pick_send_sem.at[micro])
        wait_bytes(hidden_rows.at[micro, :, pl.ds(0, replicas - 1)], hidden_send_sem.at[micro])
        wait_bytes(block_rows.at[micro, :, pl.ds(0, replicas - 1)], block_send_sem.at[micro])

        @pl.when(jnp.logical_not(is_bottom))
        def _():
            wait_bytes(token_now.at[micro], token_send_sem.at[micro])

        @pl.when(jnp.logical_not(is_bottom | adds_own))
        def _():
            wait_bytes(back_send.at[micro], back_send_sem.at[micro])

        @pl.when(adds_own)
        def _():
            wait_bytes(back_send.at[micro, :, :, pl.ds(0, experts - 1)], back_send_sem.at[micro])

        return carry

    lax.fori_loop(0, M, settle, 0)

    @pl.when(jnp.logical_not(is_bottom))
    def _():
        below_copy.wait_send()

    @pl.when(is_lower)
    def _():
        for copy in mirror_copies:
            copy.wait_send()


def row_orders(experts, capacity):
    slots = experts * capacity
    order = np.zeros((PARTS * slots, PARTS * slots), np.float32)
    for part in range(PARTS):
        for source in range(experts):
            for slot in range(capacity):
                order[
                    part * slots + source * capacity + slot,
                    (source * PARTS + part) * capacity + slot,
                ] = 1.0
    return order


def pick_tables(routes, probs, capacity):
    picks = T_MB * TOP
    flat = routes.reshape(M, picks)
    index = jnp.arange(picks, dtype=jnp.int32)
    earlier = index[None, :] < index[:, None]
    same = flat[:, :, None] == flat[:, None, :]
    position = jnp.sum((same & earlier[None]).astype(jnp.int32), axis=2)
    base = (flat * (PARTS * capacity) + position).reshape(M, T_MB, TOP).transpose(0, 2, 1)
    offset = jnp.arange(PARTS, dtype=jnp.int32) * capacity
    target = (base[:, :, None, :] + offset[None, None, :, None]).reshape(M, TOP, PARTS * T_MB)
    weight = jnp.broadcast_to(
        probs.reshape(M, T_MB, TOP).transpose(0, 2, 1)[:, :, None, :], (M, TOP, PARTS, T_MB)
    ).reshape(M, TOP, PARTS * T_MB)
    return target, weight


def per_device(adjoint_out, gate_probs, routes, saved, w_gate, w_up, w_down, probe):
    stages = lax.axis_size("pipe")
    experts = lax.axis_size("expert")
    replicas = lax.axis_size("dp")
    slots = saved.shape[5]
    capacity = slots // experts
    model = adjoint_out.shape[1]
    width = w_gate.shape[3]
    lanes = model // PARTS // CHUNKS
    wire = PARTS * capacity
    tokens = PARTS * T_MB
    block = CHUNKS * PARTS // replicas * slots
    target, weight = pick_tables(routes[0], gate_probs[0], capacity)
    order = row_orders(experts, capacity)
    vmem = pl.BlockSpec(memory_space=pltpu.VMEM)
    dma = pltpu.SemaphoreType.DMA
    found = pl.pallas_call(
        functools.partial(relay_kernel, (stages, experts, replicas, capacity)),
        out_shape=jax.ShapeDtypeStruct((model // replicas, width), F32),
        in_specs=[vmem] * 10,
        out_specs=vmem,
        scratch_shapes=[
            pltpu.VMEM((M, TOP, tokens), jnp.int32),
            pltpu.VMEM((M, TOP, tokens), F32),
            pltpu.VMEM((M, TOP, tokens), jnp.int32),
            pltpu.VMEM((M, KINDS, CHUNKS, tokens, lanes), BF16),
            pltpu.VMEM((M, KINDS, CHUNKS, tokens, lanes), BF16),
            pltpu.VMEM((M, KINDS, CHUNKS, experts, wire, lanes), BF16),
            pltpu.VMEM((M, KINDS, CHUNKS, experts, wire, lanes), BF16),
            pltpu.VMEM((M, KINDS, CHUNKS, experts, wire, lanes), BF16),
            pltpu.VMEM((M, KINDS, CHUNKS, experts, wire, lanes), BF16),
            pltpu.VMEM((M, KINDS, CHUNKS, PARTS * slots, lanes), BF16),
            pltpu.VMEM((M, KINDS, replicas, block, lanes), BF16),
            pltpu.VMEM((M, KINDS, replicas, slots, width), BF16),
            pltpu.VMEM((4, slots, width), F32),
            pltpu.VMEM((2, slots, width), F32),
            pltpu.VMEM((model // replicas, width), F32),
            pltpu.VMEM((model, width), BF16),
            pltpu.VMEM((2 * width, model), BF16),
            pltpu.VMEM((experts * wire, tokens), BF16),
            pltpu.VMEM((experts * wire, tokens), BF16),
            pltpu.VMEM((experts * wire, lanes), F32),
            dma((3,)),
            dma((3,)),
            dma((M,)),
            dma((M, KINDS, CHUNKS)),
            dma((M,)),
            dma((M, KINDS, CHUNKS)),
            dma((M,)),
            dma((M, KINDS, CHUNKS)),
            dma((M,)),
            dma((M, KINDS)),
            dma((M,)),
            dma((M,)),
        ],
        compiler_params=pltpu.CompilerParams(
            collective_id=0, has_side_effects=True, vmem_limit_bytes=60 * 1024 * 1024
        ),
        name="relay",
    )(
        target,
        weight,
        jnp.asarray(order, BF16),
        jnp.asarray(order.T, BF16),
        adjoint_out,
        saved[0, 0, 0],
        w_gate[0, 0],
        w_up[0, 0],
        w_down[0, 0],
        probe[0, 0],
    )
    return found[None, None]


def solution(mesh):
    return jax.shard_map(
        per_device,
        mesh=mesh,
        in_specs=(
            P(("expert", "dp"), None),
            P("pipe", ("expert", "dp"), None),
            P("pipe", ("expert", "dp"), None),
            P("pipe", "expert", "dp", None, None, None, None),
            P("pipe", "expert", None, None),
            P("pipe", "expert", None, None),
            P("pipe", "expert", None, None),
            P("pipe", "expert", None, None),
        ),
        out_specs=P("pipe", "expert", "dp", None),
        check_vma=False,
    )
```

```python
import functools

import jax
import jax.numpy as jnp
import numpy as np
from jax import lax
from jax.experimental import pallas as pl
from jax.experimental.pallas import tpu as pltpu
from jax.sharding import PartitionSpec as P

M = 8
T_MB = 16
TOP = 2
KINDS = 2
CHUNKS = 2
PARTS = 4
MESH = pl.DeviceIdType.MESH
F32 = jnp.float32
BF16 = jnp.bfloat16


def dot(left, right, dims):
    return lax.dot_general(left, right, (dims, ((), ())), preferred_element_type=F32)


def partner_order(experts):
    half, quarter = experts // 2, experts // 4
    if quarter == 0:
        return list(range(experts - 1, -1, -1))
    far = list(range(experts - 1, half - 1, -1))
    near = list(range(half - 1, -1, -1))
    return far[:quarter] + near[:quarter] + far[quarter:] + near[quarter:]


def wait_bytes(view, sem):
    pltpu.make_async_copy(view, view, sem).wait()


def relay_kernel(
    sizes,
    routes_ref,
    probs_ref,
    order_ref,
    unorder_ref,
    adjoint_far,
    saved_far,
    gate_far,
    up_far,
    down_far,
    probe_far,
    out_ref,
    adjoint_ref,
    saved_ref,
    gate_ref,
    up_ref,
    down_ref,
    probe_ref,
    target_ref,
    weight_ref,
    target_own,
    weight_own,
    target_above,
    token_in,
    token_now,
    pick_send,
    pick_recv,
    back_send,
    back_recv,
    pick_rows,
    block_rows,
    hidden_rows,
    factors,
    grads,
    total,
    down_turned,
    inner_turned,
    placing_ref,
    merging_ref,
    scale_ref,
    load_sem,
    table_send_sem,
    table_recv_sem,
    token_send_sem,
    token_recv_sem,
    pick_send_sem,
    pick_recv_sem,
    back_send_sem,
    back_recv_sem,
    block_send_sem,
    block_recv_sem,
    hidden_send_sem,
    hidden_recv_sem,
):
    stages, experts, replicas, capacity = sizes
    stage = lax.axis_index("pipe")
    expert = lax.axis_index("expert")
    replica = lax.axis_index("dp")
    below = lax.rem(stage + stages - 1, stages)
    above = lax.rem(stage + 1, stages)
    is_top = stage == stages - 1
    is_bottom = stage == 0
    adds_own = stage == stages // 2
    gets_sums = stage == stages // 2 - 1
    is_late = stage > stages // 2
    ends_apart = stage >= stages // 2 - 1
    back_stage = jnp.where(adds_own, stage, below)
    is_lower = stage < stages // 2
    mirror = experts - 1 - expert
    source = jnp.where(is_lower, mirror, expert)
    expert_below = jnp.where(adds_own, mirror, expert)
    slots = experts * capacity
    wire = PARTS * capacity
    lanes = pick_send.shape[-1]
    span = PARTS * lanes
    width = gate_ref.shape[1]
    block_parts = CHUNKS * PARTS // replicas
    block = block_parts * slots

    loads = [
        pltpu.make_async_copy(far, near, load_sem.at[index])
        for index, (far, near) in enumerate(
            [
                (adjoint_far, adjoint_ref),
                (down_far, down_ref),
                (gate_far, gate_ref),
                (up_far, up_ref),
                (saved_far, saved_ref),
                (probe_far, probe_ref),
            ]
        )
    ]
    for load in loads:
        load.start()

    expert_peers = [expert ^ k for k in partner_order(experts)]
    replica_peers = [lax.rem(replica + step, replicas) for step in range(replicas)]

    barrier = pltpu.get_barrier_semaphore()

    def greet(peer, carry):
        for other in (below, above):
            pl.semaphore_signal(
                barrier, inc=1, device_id={"pipe": other, "expert": peer}, device_id_type=MESH
            )
        return carry

    lax.fori_loop(0, experts, greet, 0)
    for step in range(experts - 1):
        pl.semaphore_signal(
            barrier,
            inc=1,
            device_id={"expert": expert_peers[step]},
            device_id_type=MESH,
        )
    for step in range(1, replicas):
        pl.semaphore_signal(
            barrier,
            inc=1,
            device_id={"dp": replica_peers[step]},
            device_id_type=MESH,
        )
    set_tables(routes_ref, probs_ref, target_ref, weight_ref, capacity)
    pl.semaphore_wait(barrier, 2 * experts + experts - 1 + replicas - 1)

    def table_copy(source_ref, landing_ref, index, device):
        return pltpu.make_async_remote_copy(
            src_ref=source_ref,
            dst_ref=landing_ref,
            send_sem=table_send_sem.at[index],
            recv_sem=table_recv_sem.at[index],
            device_id=device,
            device_id_type=MESH,
        )

    below_copy = table_copy(
        target_ref,
        target_above,
        0,
        {"pipe": below, "expert": jnp.where(stage <= stages // 2, mirror, expert)},
    )
    mirror_copies = [
        table_copy(target_ref, target_own, 1, {"expert": mirror}),
        table_copy(weight_ref, weight_own, 2, {"expert": mirror}),
    ]

    @pl.when(jnp.logical_not(is_bottom))
    def _():
        below_copy.start()

    @pl.when(is_lower)
    def _():
        for copy in mirror_copies:
            copy.start()
        for copy in mirror_copies:
            copy.wait_recv()

    @pl.when(jnp.logical_not(is_lower))
    def _():
        target_own[...] = target_ref[...]
        weight_own[...] = weight_ref[...]

    @pl.when(jnp.logical_not(is_top))
    def _():
        below_copy.wait_recv()

    rows = lax.broadcasted_iota(jnp.int32, (experts * wire, PARTS * T_MB), 0)

    def matches(table, micro):
        here = pl.ds(micro, 1)
        return rows == table[0, here, :], rows == table[1, here, :]

    def onehot(first, second):
        return jnp.where(first | second, 1.0, 0.0).astype(BF16)

    def curvature(micro, kind):
        if kind == 0:
            wait_bytes(hidden_rows.at[micro, :, pl.ds(0, replicas - 1)], hidden_recv_sem.at[micro])
        wait_bytes(block_rows.at[micro, kind], block_recv_sem.at[micro, kind])
        right = hidden_rows[micro, kind].reshape(replicas * slots, width)
        for part in range(block_parts):
            left = block_rows[micro, kind, :, part * slots : (part + 1) * slots, :]
            found = dot(left.reshape(replicas * slots, lanes), right, ((0,), (0,)))
            here = slice(part * lanes, (part + 1) * lanes)
            total[here, :] = total[here, :] + found

    def merge(merging, base, micro, kind, chunk):
        wait_bytes(back_recv.at[micro, kind, chunk], back_recv_sem.at[micro, kind, chunk])
        returned = back_recv[micro, kind, chunk].reshape(experts * wire, lanes)
        token_now[micro, kind, chunk] = (
            base.astype(F32) + dot(merging, returned, ((0,), (0,)))
        ).astype(BF16)

    def forward(micro, kind, chunk):
        pltpu.make_async_remote_copy(
            src_ref=token_now.at[micro, kind, chunk],
            dst_ref=token_in.at[micro, kind, chunk],
            send_sem=token_send_sem.at[micro],
            recv_sem=token_recv_sem.at[micro, kind, chunk],
            device_id={"pipe": below, "expert": expert_below},
            device_id_type=MESH,
        ).start()

    def add_own(micro, kind):
        merging = onehot(*matches(target_own, micro))
        for chunk in range(CHUNKS):
            merge(merging, token_now[micro, kind, chunk], micro, kind, chunk)
            forward(micro, kind, chunk)

    def tables(micro):
        first, second = matches(target_own, micro)
        here = pl.ds(micro, 1)
        placing_ref[...] = onehot(first, second)
        scale_ref[...] = jnp.broadcast_to(
            jnp.sum(
                jnp.where(first, weight_own[0, here, :], 0.0)
                + jnp.where(second, weight_own[1, here, :], 0.0),
                axis=1,
                keepdims=True,
            ),
            scale_ref.shape,
        )
        merging_ref[...] = onehot(*matches(target_above, micro))

    def send_picks(micro, kind, chunk):
        picked = dot(placing_ref[...], token_now[micro, kind, chunk], ((1,), (0,)))
        picked = picked * scale_ref[...]
        pick_send[micro, kind, chunk] = picked.astype(BF16).reshape(experts, wire, lanes)
        for step in range(experts - 1):
            peer = expert_peers[step]
            pltpu.make_async_remote_copy(
                src_ref=pick_send.at[micro, kind, chunk, peer],
                dst_ref=pick_recv.at[micro, kind, chunk, source],
                send_sem=pick_send_sem.at[micro],
                recv_sem=pick_recv_sem.at[micro, kind, chunk],
                device_id={"expert": peer},
                device_id_type=MESH,
            ).start()
        pltpu.make_async_copy(
            pick_send.at[micro, kind, chunk, expert],
            pick_recv.at[micro, kind, chunk, source],
            pick_recv_sem.at[micro, kind, chunk],
        ).start()

    def hand_out(micro, kind):
        for chunk in range(CHUNKS):

            @pl.when(is_top)
            def _():
                row_start = pl.multiple_of(micro * T_MB, T_MB)
                for part in range(PARTS):
                    start = chunk * span + part * lanes
                    base = part * T_MB
                    if kind == 0:
                        piece = adjoint_ref[pl.ds(row_start, T_MB), start : start + lanes]
                    else:
                        piece = jnp.zeros((T_MB, lanes), BF16)
                    token_now[micro, kind, chunk, base : base + T_MB, :] = piece

            @pl.when(jnp.logical_not(is_top))
            def _():
                wait_bytes(token_in.at[micro, kind, chunk], token_recv_sem.at[micro, kind, chunk])

            @pl.when(gets_sums)
            def _():
                token_now[micro, kind, chunk] = token_in[micro, kind, chunk]

            @pl.when(jnp.logical_not(is_top | gets_sums))
            def _():
                merge(merging_ref[...], token_in[micro, kind, chunk], micro, kind, chunk)

            if kind == 0:
                send_picks(micro, kind, chunk)
            else:
                pl.when(jnp.logical_not(is_top))(
                    functools.partial(send_picks, micro, kind, chunk)
                )

            @pl.when(jnp.logical_not(is_bottom | adds_own))
            def _():
                forward(micro, kind, chunk)

    def activations(micro):
        pre_gate = saved_ref[micro, 0].astype(F32)
        pre_up = saved_ref[micro, 1].astype(F32)
        tangent_gate = saved_ref[micro, 2].astype(F32)
        tangent_up = saved_ref[micro, 3].astype(F32)
        sigmoid = jax.nn.sigmoid(pre_gate)
        silu = pre_gate * sigmoid
        slope = sigmoid * (1.0 + pre_gate * (1.0 - sigmoid))
        return pre_gate, pre_up, tangent_gate, tangent_up, sigmoid, silu, slope

    def share_hidden(micro, carry):
        _, pre_up, tangent_gate, tangent_up, _, silu, slope = activations(micro)
        hidden_rows[micro, 0, replica] = (
            slope * tangent_gate * pre_up + silu * tangent_up
        ).astype(BF16)
        hidden_rows[micro, 1, replica] = (silu * pre_up).astype(BF16)
        for step in range(1, replicas):
            pltpu.make_async_remote_copy(
                src_ref=hidden_rows.at[micro, :, replica],
                dst_ref=hidden_rows.at[micro, :, replica],
                send_sem=hidden_send_sem.at[micro],
                recv_sem=hidden_recv_sem.at[micro],
                device_id={"dp": replica_peers[step]},
                device_id_type=MESH,
            ).start()
        return carry

    def set_factors(micro):
        pre_gate, pre_up, tangent_gate, tangent_up, sigmoid, silu, slope = activations(micro)
        bend = sigmoid * (1.0 - sigmoid) * (2.0 + pre_gate * (1.0 - 2.0 * sigmoid))
        factors[0] = pre_up * slope
        factors[1] = silu
        factors[2] = tangent_up * slope + pre_up * bend * tangent_gate
        factors[3] = slope * tangent_gate

    def side_by_side(ordered):
        return jnp.concatenate(
            [ordered[part * slots : (part + 1) * slots, :] for part in range(PARTS)], axis=1
        )

    def take_in(micro, kind):
        for chunk in range(CHUNKS):
            if kind == 0:
                take_chunk(micro, kind, chunk)
            else:
                pl.when(jnp.logical_not(is_top))(
                    functools.partial(take_chunk, micro, kind, chunk)
                )

                @pl.when(is_top)
                def _():
                    pick_rows[micro, kind, chunk] = jnp.zeros((PARTS * slots, lanes), BF16)

    def take_chunk(micro, kind, chunk):
        columns = slice(chunk * span, (chunk + 1) * span)
        wait_bytes(pick_recv.at[micro, kind, chunk], pick_recv_sem.at[micro, kind, chunk])
        received = pick_recv[micro, kind, chunk].reshape(experts * wire, lanes)
        ordered = dot(order_ref[...], received, ((1,), (0,))).astype(BF16)
        pick_rows[micro, kind, chunk] = ordered

        @pl.when(is_bottom)
        def _():
            share_rows(micro, kind, chunk)

        @pl.when(jnp.logical_not(is_bottom))
        def _():
            main = dot(side_by_side(ordered), down_turned[columns, :], ((1,), (0,)))
            if chunk == 0:
                grads[kind] = main + grads[1] if kind == 1 else main
            else:
                grads[kind] = grads[kind] + main

    def share_rows(micro, kind, chunk):
        for step in range(replicas):
            peer = replica_peers[step]
            first_part = peer * block_parts
            rows_out = pick_rows.at[
                micro, kind, chunk, pl.ds(lax.rem(first_part, PARTS) * slots, block)
            ]
            landing = block_rows.at[micro, kind, replica]

            @pl.when(lax.div(first_part, PARTS) == chunk)
            def _():
                if step == 0:
                    pltpu.make_async_copy(
                        rows_out, landing, block_recv_sem.at[micro, kind]
                    ).start()
                else:
                    pltpu.make_async_remote_copy(
                        src_ref=rows_out,
                        dst_ref=landing,
                        send_sem=block_send_sem.at[micro],
                        recv_sem=block_recv_sem.at[micro, kind],
                        device_id={"dp": peer},
                        device_id_type=MESH,
                    ).start()

    def share_all_rows(micro):
        for kind in range(KINDS):
            for chunk in range(CHUNKS):
                share_rows(micro, kind, chunk)

    def hand_back(micro, kind):
        grad = grads[0]
        if kind == 0:
            left = [grad * factors[0], grad * factors[1]]
        else:
            grad_dot = grads[1]
            left = [
                grad_dot * factors[0] + grad * factors[2],
                grad_dot * factors[1] + grad * factors[3],
            ]
        left = jnp.concatenate([piece.astype(BF16) for piece in left], axis=1)
        for chunk in range(CHUNKS):
            columns = slice(chunk * span, (chunk + 1) * span)
            back = dot(left, inner_turned[:, columns], ((1,), (0,))).astype(BF16)
            stacked = jnp.concatenate(
                [back[:, part * lanes : (part + 1) * lanes] for part in range(PARTS)], axis=0
            )
            back_send[micro, kind, chunk] = (
                dot(unorder_ref[...], stacked, ((1,), (0,)))
                .astype(BF16)
                .reshape(experts, wire, lanes)
            )
            for step in range(experts):
                peer = expert_peers[step]
                copy = pltpu.make_async_remote_copy(
                    src_ref=back_send.at[
                        micro, kind, chunk, jnp.where(is_lower, experts - 1 - peer, peer)
                    ],
                    dst_ref=back_recv.at[micro, kind, chunk, expert],
                    send_sem=back_send_sem.at[micro],
                    recv_sem=back_recv_sem.at[micro, kind, chunk],
                    device_id={"pipe": back_stage, "expert": peer},
                    device_id_type=MESH,
                )
                if step < experts - 1:
                    copy.start()
                else:
                    pl.when(jnp.logical_not(adds_own))(copy.start)

                    @pl.when(adds_own)
                    def _():
                        pltpu.make_async_copy(
                            back_send.at[micro, kind, chunk, expert],
                            back_recv.at[micro, kind, chunk, expert],
                            back_recv_sem.at[micro, kind, chunk],
                        ).start()

    total[...] = jnp.zeros_like(total)

    def turn_weights():
        for load in loads[1:]:
            load.wait()
        side = min(256, down_ref.shape[1])

        def turn_down(index, carry):
            here = pl.ds(pl.multiple_of(index * side, side), side)
            down_turned[here, :] = down_ref[:, here].T
            inner_turned[0:width, here] = gate_ref[here, :].T
            inner_turned[width : 2 * width, here] = up_ref[here, :].T
            return carry

        lax.fori_loop(0, down_ref.shape[1] // side, turn_down, 0)

    def aside(micro):
        for chunk in range(CHUNKS):
            found = dot(
                side_by_side(pick_rows[micro, 0, chunk]),
                probe_ref[chunk * span : (chunk + 1) * span, :],
                ((1,), (0,)),
            )
            grads[1] = found if chunk == 0 else grads[1] + found

    def advance(micro, carry):
        hand_out(micro, 0)
        hand_out(micro, 1)

        @pl.when(is_top & (micro == 0))
        def _():
            turn_weights()

        set_factors(micro)

        @pl.when((micro > 0) & jnp.logical_not(ends_apart))
        def _():
            curvature(micro - 1, 0)
            curvature(micro - 1, 1)

        @pl.when(micro < M - 1)
        def _():
            tables(micro + 1)

        take_in(micro, 0)

        @pl.when(jnp.logical_not(is_bottom))
        def _():
            hand_back(micro, 0)
            aside(micro)

        @pl.when(is_bottom & (micro == M - 1))
        def _():
            curvature(micro, 0)

        take_in(micro, 1)

        @pl.when(jnp.logical_not(is_bottom))
        def _():
            hand_back(micro, 1)

        @pl.when(jnp.logical_not(is_bottom | ends_apart))
        def _():
            share_all_rows(micro)

        @pl.when(adds_own)
        def _():
            add_own(micro, 0)
            add_own(micro, 1)

        return carry

    tables(0)
    loads[0].wait()

    @pl.when(jnp.logical_not(is_top))
    def _():
        turn_weights()

    @pl.when(jnp.logical_not(is_late))
    def _():
        lax.fori_loop(0, M, share_hidden, 0)

    lax.fori_loop(0, M, advance, 0)

    @pl.when(is_late)
    def _():
        lax.fori_loop(0, M, share_hidden, 0)

    @pl.when(ends_apart)
    def _():
        def share_late(micro, carry):
            share_all_rows(micro)
            return carry

        def add_late(micro, carry):
            curvature(micro, 0)
            curvature(micro, 1)
            return carry

        lax.fori_loop(0, M, share_late, 0)
        lax.fori_loop(0, M, add_late, 0)

    @pl.when(jnp.logical_not(is_bottom | ends_apart))
    def _():
        curvature(M - 1, 0)

    @pl.when(jnp.logical_not(ends_apart))
    def _():
        curvature(M - 1, 1)

    rows_here = block_parts * lanes
    start = pl.multiple_of(replica * rows_here, rows_here)
    out_ref[...] = probe_ref[pl.ds(start, rows_here), :].astype(F32) * total[...]

    def settle(micro, carry):
        @pl.when(is_top)
        def _():
            wait_bytes(pick_send.at[micro, 0, :, pl.ds(0, experts - 1)], pick_send_sem.at[micro])

        @pl.when(jnp.logical_not(is_top))
        def _():
            wait_bytes(pick_send.at[micro, :, :, pl.ds(0, experts - 1)], pick_send_sem.at[micro])

        wait_bytes(hidden_rows.at[micro, :, pl.ds(0, replicas - 1)], hidden_send_sem.at[micro])
        wait_bytes(block_rows.at[micro, :, pl.ds(0, replicas - 1)], block_send_sem.at[micro])

        @pl.when(jnp.logical_not(is_bottom))
        def _():
            wait_bytes(token_now.at[micro], token_send_sem.at[micro])

        @pl.when(jnp.logical_not(is_bottom | adds_own))
        def _():
            wait_bytes(back_send.at[micro], back_send_sem.at[micro])

        @pl.when(adds_own)
        def _():
            wait_bytes(back_send.at[micro, :, :, pl.ds(0, experts - 1)], back_send_sem.at[micro])

        return carry

    lax.fori_loop(0, M, settle, 0)

    @pl.when(jnp.logical_not(is_bottom))
    def _():
        below_copy.wait_send()

    @pl.when(is_lower)
    def _():
        for copy in mirror_copies:
            copy.wait_send()


def row_orders(experts, capacity):
    slots = experts * capacity
    order = np.zeros((PARTS * slots, PARTS * slots), np.float32)
    for part in range(PARTS):
        for source in range(experts):
            for slot in range(capacity):
                order[
                    part * slots + source * capacity + slot,
                    (source * PARTS + part) * capacity + slot,
                ] = 1.0
    return order


def set_tables(routes_ref, probs_ref, target_ref, weight_ref, capacity):
    count = M * T_MB
    across = lax.broadcasted_iota(jnp.int32, (count, count), 1)
    down = lax.broadcasted_iota(jnp.int32, (count, count), 0)
    same = across == down
    shift = T_MB.bit_length() - 1
    earlier = (down < across) & ((down >> shift) == (across >> shift))

    def row_of(column):
        return jnp.sum(jnp.where(same, column, 0.0), axis=0, keepdims=True)

    columns = [routes_ref[:, k : k + 1].astype(F32) for k in range(TOP)]
    rows = [row_of(column) for column in columns]
    wide = (M, count)
    own = (lax.broadcasted_iota(jnp.int32, wide, 1) >> shift) == lax.broadcasted_iota(
        jnp.int32, wide, 0
    )
    tall = (count, PARTS * T_MB)
    spread = jnp.where(
        (lax.broadcasted_iota(jnp.int32, tall, 0) & (T_MB - 1))
        == (lax.broadcasted_iota(jnp.int32, tall, 1) & (T_MB - 1)),
        1.0,
        0.0,
    ).astype(BF16)
    part = lax.broadcasted_iota(jnp.int32, (M, PARTS * T_MB), 1) >> shift

    def per_micro(row):
        return dot(jnp.where(own, row, 0.0).astype(BF16), spread, ((1,), (0,)))

    for k in range(TOP):
        before = sum(
            jnp.where(earlier & (column == rows[k]), 1.0, 0.0) for column in columns
        )
        position = jnp.sum(before, axis=0, keepdims=True)
        for other in range(k):
            position = position + jnp.where(rows[other] == rows[k], 1.0, 0.0)
        base = per_micro(rows[k] * (PARTS * capacity) + position)
        target_ref[k] = base.astype(jnp.int32) + part * capacity
        weight = row_of(probs_ref[:, k : k + 1])
        high = weight.astype(BF16).astype(F32)
        middle = (weight - high).astype(BF16).astype(F32)
        low = weight - high - middle
        weight_ref[k] = per_micro(high) + per_micro(middle) + per_micro(low)


def per_device(adjoint_out, gate_probs, routes, saved, w_gate, w_up, w_down, probe):
    stages = lax.axis_size("pipe")
    experts = lax.axis_size("expert")
    replicas = lax.axis_size("dp")
    slots = saved.shape[5]
    capacity = slots // experts
    model = adjoint_out.shape[1]
    width = w_gate.shape[3]
    lanes = model // PARTS // CHUNKS
    wire = PARTS * capacity
    tokens = PARTS * T_MB
    block = CHUNKS * PARTS // replicas * slots
    order = row_orders(experts, capacity)
    vmem = pl.BlockSpec(memory_space=pltpu.VMEM)
    dma = pltpu.SemaphoreType.DMA
    found = pl.pallas_call(
        functools.partial(relay_kernel, (stages, experts, replicas, capacity)),
        out_shape=jax.ShapeDtypeStruct((model // replicas, width), F32),
        in_specs=[vmem] * 4 + [pl.BlockSpec(memory_space=pl.ANY)] * 6,
        out_specs=vmem,
        scratch_shapes=[
            pltpu.VMEM(adjoint_out.shape, BF16),
            pltpu.VMEM(saved.shape[3:], BF16),
            pltpu.VMEM((model, width), BF16),
            pltpu.VMEM((model, width), BF16),
            pltpu.VMEM((width, model), BF16),
            pltpu.VMEM((model, width), BF16),
            pltpu.VMEM((TOP, M, tokens), jnp.int32),
            pltpu.VMEM((TOP, M, tokens), F32),
            pltpu.VMEM((TOP, M, tokens), jnp.int32),
            pltpu.VMEM((TOP, M, tokens), F32),
            pltpu.VMEM((TOP, M, tokens), jnp.int32),
            pltpu.VMEM((M, KINDS, CHUNKS, tokens, lanes), BF16),
            pltpu.VMEM((M, KINDS, CHUNKS, tokens, lanes), BF16),
            pltpu.VMEM((M, KINDS, CHUNKS, experts, wire, lanes), BF16),
            pltpu.VMEM((M, KINDS, CHUNKS, experts, wire, lanes), BF16),
            pltpu.VMEM((M, KINDS, CHUNKS, experts, wire, lanes), BF16),
            pltpu.VMEM((M, KINDS, CHUNKS, experts, wire, lanes), BF16),
            pltpu.VMEM((M, KINDS, CHUNKS, PARTS * slots, lanes), BF16),
            pltpu.VMEM((M, KINDS, replicas, block, lanes), BF16),
            pltpu.VMEM((M, KINDS, replicas, slots, width), BF16),
            pltpu.VMEM((4, slots, width), F32),
            pltpu.VMEM((2, slots, width), F32),
            pltpu.VMEM((model // replicas, width), F32),
            pltpu.VMEM((model, width), BF16),
            pltpu.VMEM((2 * width, model), BF16),
            pltpu.VMEM((experts * wire, tokens), BF16),
            pltpu.VMEM((experts * wire, tokens), BF16),
            pltpu.VMEM((experts * wire, lanes), F32),
            dma((6,)),
            dma((3,)),
            dma((3,)),
            dma((M,)),
            dma((M, KINDS, CHUNKS)),
            dma((M,)),
            dma((M, KINDS, CHUNKS)),
            dma((M,)),
            dma((M, KINDS, CHUNKS)),
            dma((M,)),
            dma((M, KINDS)),
            dma((M,)),
            dma((M,)),
        ],
        compiler_params=pltpu.CompilerParams(
            collective_id=0, has_side_effects=True, vmem_limit_bytes=60 * 1024 * 1024
        ),
        name="relay",
    )(
        routes[0],
        gate_probs[0],
        jnp.asarray(order, BF16),
        jnp.asarray(order.T, BF16),
        adjoint_out,
        saved[0, 0, 0],
        w_gate[0, 0],
        w_up[0, 0],
        w_down[0, 0],
        probe[0, 0],
    )
    return found[None, None]


def solution(mesh):
    return jax.shard_map(
        per_device,
        mesh=mesh,
        in_specs=(
            P(("expert", "dp"), None),
            P("pipe", ("expert", "dp"), None),
            P("pipe", ("expert", "dp"), None),
            P("pipe", "expert", "dp", None, None, None, None),
            P("pipe", "expert", None, None),
            P("pipe", "expert", None, None),
            P("pipe", "expert", None, None),
            P("pipe", "expert", None, None),
        ),
        out_specs=P("pipe", "expert", "dp", None),
        check_vma=False,
    )
```

```python
import functools

import jax
import jax.numpy as jnp
import numpy as np
from jax import lax
from jax.experimental import pallas as pl
from jax.experimental.pallas import tpu as pltpu
from jax.sharding import PartitionSpec as P

M = 8
T_MB = 16
TOP = 2
KINDS = 2
CHUNKS = 2
PARTS = 4
MESH = pl.DeviceIdType.MESH
F32 = jnp.float32
BF16 = jnp.bfloat16


def dot(left, right, dims):
    return lax.dot_general(left, right, (dims, ((), ())), preferred_element_type=F32)


def partner_order(experts):
    half, quarter = experts // 2, experts // 4
    if quarter == 0:
        return list(range(experts - 1, -1, -1))
    far = list(range(experts - 1, half - 1, -1))
    near = list(range(half - 1, -1, -1))
    return far[:quarter] + near[:quarter] + far[quarter:] + near[quarter:]


def wait_bytes(view, sem):
    pltpu.make_async_copy(view, view, sem).wait()


def relay_kernel(
    sizes,
    routes_ref,
    probs_ref,
    order_ref,
    unorder_ref,
    adjoint_far,
    saved_far,
    gate_far,
    up_far,
    down_far,
    probe_far,
    out_ref,
    adjoint_ref,
    saved_ref,
    gate_ref,
    up_ref,
    down_ref,
    probe_ref,
    target_ref,
    weight_ref,
    target_own,
    weight_own,
    target_above,
    token_in,
    token_now,
    pick_send,
    pick_recv,
    back_send,
    back_recv,
    pick_rows,
    block_rows,
    hidden_rows,
    factors,
    grads,
    total,
    down_turned,
    inner_turned,
    placing_ref,
    merging_ref,
    scale_ref,
    load_sem,
    table_send_sem,
    table_recv_sem,
    token_send_sem,
    token_recv_sem,
    pick_send_sem,
    pick_recv_sem,
    back_send_sem,
    back_recv_sem,
    block_send_sem,
    block_recv_sem,
    hidden_send_sem,
    hidden_recv_sem,
):
    stages, experts, replicas, capacity = sizes
    stage = lax.axis_index("pipe")
    expert = lax.axis_index("expert")
    replica = lax.axis_index("dp")
    below = lax.rem(stage + stages - 1, stages)
    above = lax.rem(stage + 1, stages)
    is_top = stage == stages - 1
    is_bottom = stage == 0
    adds_own = stage == stages // 2
    gets_sums = stage == stages // 2 - 1
    is_late = stage > stages // 2
    ends_apart = stage >= stages // 2 - 1
    back_stage = jnp.where(adds_own, stage, below)
    is_lower = stage < stages // 2
    mirror = experts - 1 - expert
    source = jnp.where(is_lower, mirror, expert)
    expert_below = jnp.where(adds_own, mirror, expert)
    slots = experts * capacity
    wire = PARTS * capacity
    lanes = pick_send.shape[-1]
    span = PARTS * lanes
    width = gate_ref.shape[1]
    block_parts = CHUNKS * PARTS // replicas
    block = block_parts * slots

    loads = [
        pltpu.make_async_copy(far, near, load_sem.at[index])
        for index, (far, near) in enumerate(
            [
                (adjoint_far, adjoint_ref),
                (down_far, down_ref),
                (gate_far, gate_ref),
                (up_far, up_ref),
                (saved_far, saved_ref),
                (probe_far, probe_ref),
            ]
        )
    ]
    for load in loads:
        load.start()

    expert_peers = [expert ^ k for k in partner_order(experts)]
    replica_peers = [lax.rem(replica + step, replicas) for step in range(replicas)]

    barrier = pltpu.get_barrier_semaphore()

    def greet(peer, carry):
        for other in (below, above):
            pl.semaphore_signal(
                barrier, inc=1, device_id={"pipe": other, "expert": peer}, device_id_type=MESH
            )
        return carry

    lax.fori_loop(0, experts, greet, 0)
    for step in range(experts - 1):
        pl.semaphore_signal(
            barrier,
            inc=1,
            device_id={"expert": expert_peers[step]},
            device_id_type=MESH,
        )
    for step in range(1, replicas):
        pl.semaphore_signal(
            barrier,
            inc=1,
            device_id={"dp": replica_peers[step]},
            device_id_type=MESH,
        )
    set_tables(routes_ref, probs_ref, target_ref, weight_ref, capacity)
    pl.semaphore_wait(barrier, 2 * experts + experts - 1 + replicas - 1)

    def table_copy(source_ref, landing_ref, index, device):
        return pltpu.make_async_remote_copy(
            src_ref=source_ref,
            dst_ref=landing_ref,
            send_sem=table_send_sem.at[index],
            recv_sem=table_recv_sem.at[index],
            device_id=device,
            device_id_type=MESH,
        )

    below_copy = table_copy(
        target_ref,
        target_above,
        0,
        {"pipe": below, "expert": jnp.where(stage <= stages // 2, mirror, expert)},
    )
    mirror_copies = [
        table_copy(target_ref, target_own, 1, {"expert": mirror}),
        table_copy(weight_ref, weight_own, 2, {"expert": mirror}),
    ]

    @pl.when(jnp.logical_not(is_bottom))
    def _():
        below_copy.start()

    @pl.when(is_lower)
    def _():
        for copy in mirror_copies:
            copy.start()
        for copy in mirror_copies:
            copy.wait_recv()

    @pl.when(jnp.logical_not(is_lower))
    def _():
        target_own[...] = target_ref[...]
        weight_own[...] = weight_ref[...]

    @pl.when(jnp.logical_not(is_top))
    def _():
        below_copy.wait_recv()

    rows = lax.broadcasted_iota(jnp.int32, (experts * wire, PARTS * T_MB), 0)

    def matches(table, micro):
        here = pl.ds(micro, 1)
        return rows == table[0, here, :], rows == table[1, here, :]

    def onehot(first, second):
        return jnp.where(first | second, 1.0, 0.0).astype(BF16)

    def curvature(micro, kind):
        if kind == 0:
            wait_bytes(hidden_rows.at[micro, :, pl.ds(0, replicas - 1)], hidden_recv_sem.at[micro])
        wait_bytes(block_rows.at[micro, kind], block_recv_sem.at[micro, kind])
        right = hidden_rows[micro, kind].reshape(replicas * slots, width)
        for part in range(block_parts):
            left = block_rows[micro, kind, :, part * slots : (part + 1) * slots, :]
            found = dot(left.reshape(replicas * slots, lanes), right, ((0,), (0,)))
            here = slice(part * lanes, (part + 1) * lanes)
            total[here, :] = total[here, :] + found

    def merge(merging, base, micro, kind, chunk):
        wait_bytes(back_recv.at[micro, kind, chunk], back_recv_sem.at[micro, kind, chunk])
        returned = back_recv[micro, kind, chunk].reshape(experts * wire, lanes)
        token_now[micro, kind, chunk] = (
            base.astype(F32) + dot(merging, returned, ((0,), (0,)))
        ).astype(BF16)

    def forward(micro, kind, chunk):
        pltpu.make_async_remote_copy(
            src_ref=token_now.at[micro, kind, chunk],
            dst_ref=token_in.at[micro, kind, chunk],
            send_sem=token_send_sem.at[micro],
            recv_sem=token_recv_sem.at[micro, kind, chunk],
            device_id={"pipe": below, "expert": expert_below},
            device_id_type=MESH,
        ).start()

    def add_own(micro, kind):
        merging = onehot(*matches(target_own, micro))
        for chunk in range(CHUNKS):
            merge(merging, token_now[micro, kind, chunk], micro, kind, chunk)
            forward(micro, kind, chunk)

    def tables(micro):
        first, second = matches(target_own, micro)
        here = pl.ds(micro, 1)
        placing_ref[...] = onehot(first, second)
        scale_ref[...] = jnp.broadcast_to(
            jnp.sum(
                jnp.where(first, weight_own[0, here, :], 0.0)
                + jnp.where(second, weight_own[1, here, :], 0.0),
                axis=1,
                keepdims=True,
            ),
            scale_ref.shape,
        )
        merging_ref[...] = onehot(*matches(target_above, micro))

    def send_picks(micro, kind, chunk):
        picked = dot(placing_ref[...], token_now[micro, kind, chunk], ((1,), (0,)))
        picked = picked * scale_ref[...]
        pick_send[micro, kind, chunk] = picked.astype(BF16).reshape(experts, wire, lanes)
        for step in range(experts - 1):
            peer = expert_peers[step]
            pltpu.make_async_remote_copy(
                src_ref=pick_send.at[micro, kind, chunk, peer],
                dst_ref=pick_recv.at[micro, kind, chunk, source],
                send_sem=pick_send_sem.at[micro],
                recv_sem=pick_recv_sem.at[micro, kind, chunk],
                device_id={"expert": peer},
                device_id_type=MESH,
            ).start()
        pltpu.make_async_copy(
            pick_send.at[micro, kind, chunk, expert],
            pick_recv.at[micro, kind, chunk, source],
            pick_recv_sem.at[micro, kind, chunk],
        ).start()

    def hand_out(micro, kind):
        for chunk in range(CHUNKS):

            @pl.when(is_top)
            def _():
                row_start = pl.multiple_of(micro * T_MB, T_MB)
                for part in range(PARTS):
                    start = chunk * span + part * lanes
                    base = part * T_MB
                    if kind == 0:
                        piece = adjoint_ref[pl.ds(row_start, T_MB), start : start + lanes]
                    else:
                        piece = jnp.zeros((T_MB, lanes), BF16)
                    token_now[micro, kind, chunk, base : base + T_MB, :] = piece

            @pl.when(jnp.logical_not(is_top))
            def _():
                wait_bytes(token_in.at[micro, kind, chunk], token_recv_sem.at[micro, kind, chunk])

            @pl.when(gets_sums)
            def _():
                token_now[micro, kind, chunk] = token_in[micro, kind, chunk]

            @pl.when(jnp.logical_not(is_top | gets_sums))
            def _():
                merge(merging_ref[...], token_in[micro, kind, chunk], micro, kind, chunk)

            if kind == 0:
                send_picks(micro, kind, chunk)
            else:
                pl.when(jnp.logical_not(is_top))(
                    functools.partial(send_picks, micro, kind, chunk)
                )

        @pl.when(jnp.logical_not(is_bottom | adds_own))
        def _():
            for chunk in range(CHUNKS):
                forward(micro, kind, chunk)

    def activations(micro):
        pre_gate = saved_ref[micro, 0].astype(F32)
        pre_up = saved_ref[micro, 1].astype(F32)
        tangent_gate = saved_ref[micro, 2].astype(F32)
        tangent_up = saved_ref[micro, 3].astype(F32)
        sigmoid = jax.nn.sigmoid(pre_gate)
        silu = pre_gate * sigmoid
        slope = sigmoid * (1.0 + pre_gate * (1.0 - sigmoid))
        return pre_gate, pre_up, tangent_gate, tangent_up, sigmoid, silu, slope

    def share_hidden(micro, carry):
        _, pre_up, tangent_gate, tangent_up, _, silu, slope = activations(micro)
        hidden_rows[micro, 0, replica] = (
            slope * tangent_gate * pre_up + silu * tangent_up
        ).astype(BF16)
        hidden_rows[micro, 1, replica] = (silu * pre_up).astype(BF16)
        for step in range(1, replicas):
            pltpu.make_async_remote_copy(
                src_ref=hidden_rows.at[micro, :, replica],
                dst_ref=hidden_rows.at[micro, :, replica],
                send_sem=hidden_send_sem.at[micro],
                recv_sem=hidden_recv_sem.at[micro],
                device_id={"dp": replica_peers[step]},
                device_id_type=MESH,
            ).start()
        return carry

    def set_factors(micro):
        pre_gate, pre_up, tangent_gate, tangent_up, sigmoid, silu, slope = activations(micro)
        bend = sigmoid * (1.0 - sigmoid) * (2.0 + pre_gate * (1.0 - 2.0 * sigmoid))
        factors[0] = pre_up * slope
        factors[1] = silu
        factors[2] = tangent_up * slope + pre_up * bend * tangent_gate
        factors[3] = slope * tangent_gate

    def side_by_side(ordered):
        return jnp.concatenate(
            [ordered[part * slots : (part + 1) * slots, :] for part in range(PARTS)], axis=1
        )

    def take_in(micro, kind):
        for chunk in range(CHUNKS):
            if kind == 0:
                take_chunk(micro, kind, chunk)
            else:
                pl.when(jnp.logical_not(is_top))(
                    functools.partial(take_chunk, micro, kind, chunk)
                )

                @pl.when(is_top)
                def _():
                    pick_rows[micro, kind, chunk] = jnp.zeros((PARTS * slots, lanes), BF16)

    def take_chunk(micro, kind, chunk):
        columns = slice(chunk * span, (chunk + 1) * span)
        wait_bytes(pick_recv.at[micro, kind, chunk], pick_recv_sem.at[micro, kind, chunk])
        received = pick_recv[micro, kind, chunk].reshape(experts * wire, lanes)
        ordered = dot(order_ref[...], received, ((1,), (0,))).astype(BF16)
        pick_rows[micro, kind, chunk] = ordered

        @pl.when(is_bottom)
        def _():
            share_rows(micro, kind, chunk)

        @pl.when(jnp.logical_not(is_bottom))
        def _():
            main = dot(side_by_side(ordered), down_turned[columns, :], ((1,), (0,)))
            if chunk == 0:
                grads[kind] = main + grads[1] if kind == 1 else main
            else:
                grads[kind] = grads[kind] + main

    def share_rows(micro, kind, chunk):
        for step in range(replicas):
            peer = replica_peers[step]
            first_part = peer * block_parts
            rows_out = pick_rows.at[
                micro, kind, chunk, pl.ds(lax.rem(first_part, PARTS) * slots, block)
            ]
            landing = block_rows.at[micro, kind, replica]

            @pl.when(lax.div(first_part, PARTS) == chunk)
            def _():
                if step == 0:
                    pltpu.make_async_copy(
                        rows_out, landing, block_recv_sem.at[micro, kind]
                    ).start()
                else:
                    pltpu.make_async_remote_copy(
                        src_ref=rows_out,
                        dst_ref=landing,
                        send_sem=block_send_sem.at[micro],
                        recv_sem=block_recv_sem.at[micro, kind],
                        device_id={"dp": peer},
                        device_id_type=MESH,
                    ).start()

    def share_all_rows(micro):
        for kind in range(KINDS):
            for chunk in range(CHUNKS):
                share_rows(micro, kind, chunk)

    def hand_back(micro, kind):
        grad = grads[0]
        if kind == 0:
            left = [grad * factors[0], grad * factors[1]]
        else:
            grad_dot = grads[1]
            left = [
                grad_dot * factors[0] + grad * factors[2],
                grad_dot * factors[1] + grad * factors[3],
            ]
        left = jnp.concatenate([piece.astype(BF16) for piece in left], axis=1)
        for chunk in range(CHUNKS):
            columns = slice(chunk * span, (chunk + 1) * span)
            back = dot(left, inner_turned[:, columns], ((1,), (0,))).astype(BF16)
            stacked = jnp.concatenate(
                [back[:, part * lanes : (part + 1) * lanes] for part in range(PARTS)], axis=0
            )
            back_send[micro, kind, chunk] = (
                dot(unorder_ref[...], stacked, ((1,), (0,)))
                .astype(BF16)
                .reshape(experts, wire, lanes)
            )
            for step in range(experts):
                peer = expert_peers[step]
                copy = pltpu.make_async_remote_copy(
                    src_ref=back_send.at[
                        micro, kind, chunk, jnp.where(is_lower, experts - 1 - peer, peer)
                    ],
                    dst_ref=back_recv.at[micro, kind, chunk, expert],
                    send_sem=back_send_sem.at[micro],
                    recv_sem=back_recv_sem.at[micro, kind, chunk],
                    device_id={"pipe": back_stage, "expert": peer},
                    device_id_type=MESH,
                )
                if step < experts - 1:
                    copy.start()
                else:
                    pl.when(jnp.logical_not(adds_own))(copy.start)

                    @pl.when(adds_own)
                    def _():
                        pltpu.make_async_copy(
                            back_send.at[micro, kind, chunk, expert],
                            back_recv.at[micro, kind, chunk, expert],
                            back_recv_sem.at[micro, kind, chunk],
                        ).start()

    total[...] = jnp.zeros_like(total)

    def turn_weights():
        for load in loads[1:]:
            load.wait()
        side = min(256, down_ref.shape[1])

        def turn_down(index, carry):
            here = pl.ds(pl.multiple_of(index * side, side), side)
            down_turned[here, :] = down_ref[:, here].T
            inner_turned[0:width, here] = gate_ref[here, :].T
            inner_turned[width : 2 * width, here] = up_ref[here, :].T
            return carry

        lax.fori_loop(0, down_ref.shape[1] // side, turn_down, 0)

    def aside(micro):
        for chunk in range(CHUNKS):
            found = dot(
                side_by_side(pick_rows[micro, 0, chunk]),
                probe_ref[chunk * span : (chunk + 1) * span, :],
                ((1,), (0,)),
            )
            grads[1] = found if chunk == 0 else grads[1] + found

    def advance(micro, carry):
        hand_out(micro, 0)
        hand_out(micro, 1)

        @pl.when(is_top & (micro == 0))
        def _():
            turn_weights()

        set_factors(micro)

        @pl.when((micro > 0) & jnp.logical_not(ends_apart))
        def _():
            curvature(micro - 1, 0)
            curvature(micro - 1, 1)

        @pl.when(micro < M - 1)
        def _():
            tables(micro + 1)

        take_in(micro, 0)

        @pl.when(jnp.logical_not(is_bottom))
        def _():
            hand_back(micro, 0)
            aside(micro)

        @pl.when(is_bottom & (micro == M - 1))
        def _():
            curvature(micro, 0)

        take_in(micro, 1)

        @pl.when(jnp.logical_not(is_bottom))
        def _():
            hand_back(micro, 1)

        @pl.when(jnp.logical_not(is_bottom | ends_apart))
        def _():
            share_all_rows(micro)

        @pl.when(adds_own)
        def _():
            add_own(micro, 0)
            add_own(micro, 1)

        return carry

    tables(0)
    loads[0].wait()

    @pl.when(jnp.logical_not(is_top))
    def _():
        turn_weights()

    @pl.when(jnp.logical_not(is_late))
    def _():
        lax.fori_loop(0, M, share_hidden, 0)

    lax.fori_loop(0, M, advance, 0)

    @pl.when(is_late)
    def _():
        lax.fori_loop(0, M, share_hidden, 0)

    @pl.when(ends_apart)
    def _():
        def share_late(micro, carry):
            share_all_rows(micro)
            return carry

        def add_late(micro, carry):
            curvature(micro, 0)
            curvature(micro, 1)
            return carry

        lax.fori_loop(0, M, share_late, 0)
        lax.fori_loop(0, M, add_late, 0)

    @pl.when(jnp.logical_not(is_bottom | ends_apart))
    def _():
        curvature(M - 1, 0)

    @pl.when(jnp.logical_not(ends_apart))
    def _():
        curvature(M - 1, 1)

    rows_here = block_parts * lanes
    start = pl.multiple_of(replica * rows_here, rows_here)
    out_ref[...] = probe_ref[pl.ds(start, rows_here), :].astype(F32) * total[...]

    def settle(micro, carry):
        @pl.when(is_top)
        def _():
            wait_bytes(pick_send.at[micro, 0, :, pl.ds(0, experts - 1)], pick_send_sem.at[micro])

        @pl.when(jnp.logical_not(is_top))
        def _():
            wait_bytes(pick_send.at[micro, :, :, pl.ds(0, experts - 1)], pick_send_sem.at[micro])

        wait_bytes(hidden_rows.at[micro, :, pl.ds(0, replicas - 1)], hidden_send_sem.at[micro])
        wait_bytes(block_rows.at[micro, :, pl.ds(0, replicas - 1)], block_send_sem.at[micro])

        @pl.when(jnp.logical_not(is_bottom))
        def _():
            wait_bytes(token_now.at[micro], token_send_sem.at[micro])

        @pl.when(jnp.logical_not(is_bottom | adds_own))
        def _():
            wait_bytes(back_send.at[micro], back_send_sem.at[micro])

        @pl.when(adds_own)
        def _():
            wait_bytes(back_send.at[micro, :, :, pl.ds(0, experts - 1)], back_send_sem.at[micro])

        return carry

    lax.fori_loop(0, M, settle, 0)

    @pl.when(jnp.logical_not(is_bottom))
    def _():
        below_copy.wait_send()

    @pl.when(is_lower)
    def _():
        for copy in mirror_copies:
            copy.wait_send()


def row_orders(experts, capacity):
    slots = experts * capacity
    order = np.zeros((PARTS * slots, PARTS * slots), np.float32)
    for part in range(PARTS):
        for source in range(experts):
            for slot in range(capacity):
                order[
                    part * slots + source * capacity + slot,
                    (source * PARTS + part) * capacity + slot,
                ] = 1.0
    return order


def set_tables(routes_ref, probs_ref, target_ref, weight_ref, capacity):
    count = M * T_MB
    across = lax.broadcasted_iota(jnp.int32, (count, count), 1)
    down = lax.broadcasted_iota(jnp.int32, (count, count), 0)
    same = across == down
    shift = T_MB.bit_length() - 1
    earlier = (down < across) & ((down >> shift) == (across >> shift))

    rows = [routes_ref[k : k + 1, :].astype(F32) for k in range(TOP)]
    columns = [jnp.sum(jnp.where(same, row, 0.0), axis=1, keepdims=True) for row in rows]
    wide = (M, count)
    own = (lax.broadcasted_iota(jnp.int32, wide, 1) >> shift) == lax.broadcasted_iota(
        jnp.int32, wide, 0
    )
    tall = (count, PARTS * T_MB)
    spread = jnp.where(
        (lax.broadcasted_iota(jnp.int32, tall, 0) & (T_MB - 1))
        == (lax.broadcasted_iota(jnp.int32, tall, 1) & (T_MB - 1)),
        1.0,
        0.0,
    ).astype(BF16)
    part = lax.broadcasted_iota(jnp.int32, (M, PARTS * T_MB), 1) >> shift

    def per_micro(row):
        return dot(jnp.where(own, row, 0.0).astype(BF16), spread, ((1,), (0,)))

    for k in range(TOP):
        before = sum(
            jnp.where(earlier & (column == rows[k]), 1.0, 0.0) for column in columns
        )
        position = jnp.sum(before, axis=0, keepdims=True)
        for other in range(k):
            position = position + jnp.where(rows[other] == rows[k], 1.0, 0.0)
        base = per_micro(rows[k] * (PARTS * capacity) + position)
        target_ref[k] = base.astype(jnp.int32) + part * capacity
        weight = probs_ref[k : k + 1, :]
        high = weight.astype(BF16).astype(F32)
        middle = (weight - high).astype(BF16).astype(F32)
        low = weight - high - middle
        weight_ref[k] = per_micro(high) + per_micro(middle) + per_micro(low)


def per_device(adjoint_out, gate_probs, routes, saved, w_gate, w_up, w_down, probe):
    stages = lax.axis_size("pipe")
    experts = lax.axis_size("expert")
    replicas = lax.axis_size("dp")
    slots = saved.shape[5]
    capacity = slots // experts
    model = adjoint_out.shape[1]
    width = w_gate.shape[3]
    lanes = model // PARTS // CHUNKS
    wire = PARTS * capacity
    tokens = PARTS * T_MB
    block = CHUNKS * PARTS // replicas * slots
    order = row_orders(experts, capacity)
    vmem = pl.BlockSpec(memory_space=pltpu.VMEM)
    dma = pltpu.SemaphoreType.DMA
    found = pl.pallas_call(
        functools.partial(relay_kernel, (stages, experts, replicas, capacity)),
        out_shape=jax.ShapeDtypeStruct((model // replicas, width), F32),
        in_specs=[vmem] * 4 + [pl.BlockSpec(memory_space=pl.ANY)] * 6,
        out_specs=vmem,
        scratch_shapes=[
            pltpu.VMEM(adjoint_out.shape, BF16),
            pltpu.VMEM(saved.shape[3:], BF16),
            pltpu.VMEM((model, width), BF16),
            pltpu.VMEM((model, width), BF16),
            pltpu.VMEM((width, model), BF16),
            pltpu.VMEM((model, width), BF16),
            pltpu.VMEM((TOP, M, tokens), jnp.int32),
            pltpu.VMEM((TOP, M, tokens), F32),
            pltpu.VMEM((TOP, M, tokens), jnp.int32),
            pltpu.VMEM((TOP, M, tokens), F32),
            pltpu.VMEM((TOP, M, tokens), jnp.int32),
            pltpu.VMEM((M, KINDS, CHUNKS, tokens, lanes), BF16),
            pltpu.VMEM((M, KINDS, CHUNKS, tokens, lanes), BF16),
            pltpu.VMEM((M, KINDS, CHUNKS, experts, wire, lanes), BF16),
            pltpu.VMEM((M, KINDS, CHUNKS, experts, wire, lanes), BF16),
            pltpu.VMEM((M, KINDS, CHUNKS, experts, wire, lanes), BF16),
            pltpu.VMEM((M, KINDS, CHUNKS, experts, wire, lanes), BF16),
            pltpu.VMEM((M, KINDS, CHUNKS, PARTS * slots, lanes), BF16),
            pltpu.VMEM((M, KINDS, replicas, block, lanes), BF16),
            pltpu.VMEM((M, KINDS, replicas, slots, width), BF16),
            pltpu.VMEM((4, slots, width), F32),
            pltpu.VMEM((2, slots, width), F32),
            pltpu.VMEM((model // replicas, width), F32),
            pltpu.VMEM((model, width), BF16),
            pltpu.VMEM((2 * width, model), BF16),
            pltpu.VMEM((experts * wire, tokens), BF16),
            pltpu.VMEM((experts * wire, tokens), BF16),
            pltpu.VMEM((experts * wire, lanes), F32),
            dma((6,)),
            dma((3,)),
            dma((3,)),
            dma((M,)),
            dma((M, KINDS, CHUNKS)),
            dma((M,)),
            dma((M, KINDS, CHUNKS)),
            dma((M,)),
            dma((M, KINDS, CHUNKS)),
            dma((M,)),
            dma((M, KINDS)),
            dma((M,)),
            dma((M,)),
        ],
        compiler_params=pltpu.CompilerParams(
            collective_id=0, has_side_effects=True, vmem_limit_bytes=60 * 1024 * 1024
        ),
        name="relay",
    )(
        routes[0].T,
        gate_probs[0].T,
        jnp.asarray(order, BF16),
        jnp.asarray(order.T, BF16),
        adjoint_out,
        saved[0, 0, 0],
        w_gate[0, 0],
        w_up[0, 0],
        w_down[0, 0],
        probe[0, 0],
    )
    return found[None, None]


def solution(mesh):
    return jax.shard_map(
        per_device,
        mesh=mesh,
        in_specs=(
            P(("expert", "dp"), None),
            P("pipe", ("expert", "dp"), None),
            P("pipe", ("expert", "dp"), None),
            P("pipe", "expert", "dp", None, None, None, None),
            P("pipe", "expert", None, None),
            P("pipe", "expert", None, None),
            P("pipe", "expert", None, None),
            P("pipe", "expert", None, None),
        ),
        out_specs=P("pipe", "expert", "dp", None),
        check_vma=False,
    )
```
